256 devices in a mesh: frow: 16 (over z, x_lo), fcol: 16 (over y, x_hi, core).
Axes of the slice: x: 4 (x_hi: 2, x_lo: 2; x = x_hi * 2 + x_lo), y: 4, z: 8, core: 2. Of those that a mesh axis runs over, the one named last changes fastest.
Arguments:
- facets: float32 [2, 2048, 16384], P(None, 'frow', 'fcol'), may hold values from -6 to 6
- column_start: int32 [1], replicated, may hold values from 0 to 16383
- subgrid_start: int32 [16], replicated, may hold values from 0 to 2047
- vis_count: int32 [16], P('frow'), may hold values from 1 to 64
- vis_row: int32 [16, 64], P('frow'), may hold values from 0 to 511
- vis_weight: float32 [16, 64, 512], P('frow', None, 'fcol'), may hold values from -1 to 1
Outputs:
- corrected: float32 [16, 512, 2, 512], P('frow', 'fcol')
- facet_update: float32 [2, 2048, 16384], P(None, 'frow', 'fcol')
The draws below stay inside these ranges and needn't reach their ends.
All inputs are finite; a program needn't handle non-finite values.
Results may differ from the reference program's by a relative error of at most 0.0003.
Values sent between devices are 32-bit elements; how exact they have to be, the bound alone decides.
A program may use at most 64 MiB of HBM per device.

```python
import math
import jax
import jax.numpy as jnp
from jax import lax

SG = 512
MAXB = 64
NSUB = 16
N1 = 2048
N2 = 16384


def place_ends(values, rng, least, high):
    place = [jax.random.randint(jax.random.fold_in(rng, axis), (), 0, length) for axis, length in enumerate(values.shape)]
    main_axis = values.shape.index(max(values.shape))
    neighbour = place[:main_axis] + [(place[main_axis] + 1) % values.shape[main_axis]] + place[main_axis + 1:]
    return values.at[tuple(place)].set(least).at[tuple(neighbour)].set(high)


def steps_of(stream_key, extent, shards, low, top_value):
    level = 1.0
    for dim, shards_of in shards:
        steps = jax.random.uniform(jax.random.fold_in(jax.random.fold_in(stream_key, 6), dim), (shards_of,), jnp.float32, low / len(shards), top_value / len(shards))
        level = level * jnp.repeat(jnp.exp(steps), extent[dim] // shards_of).reshape((-1,) + (1,) * (len(extent) - 1 - dim))
    return level


def bell_draw(stream_key, shape, deviation, reach, cuts=(), held_as=jnp.bfloat16):
    loudness = steps_of(stream_key, shape, cuts, -0.22, 0.18) if cuts else 1.0
    result = jax.random.normal(stream_key, shape, jnp.float32) * deviation * loudness
    return jnp.minimum(jnp.maximum(result, -reach), reach).astype(held_as)


def setup_inputs(seed: int = 0) -> dict:
    key_of = jax.random.split(jax.random.key(seed), 7)
    facets = bell_draw(key_of[0], (2, N1, N2), 1.0, 6.0, ((1, 16), (2, 16)), jnp.float32)
    column_start = jax.random.randint(key_of[1], (1,), 0, N2).astype(jnp.int32)
    subgrid_start = place_ends(jax.random.randint(key_of[2], (NSUB,), 0, N1), jax.random.fold_in(key_of[2], 1), 0, N1 - 1).astype(jnp.int32)
    vis_count = place_ends(jax.random.randint(key_of[3], (NSUB,), 1, MAXB + 1), jax.random.fold_in(key_of[3], 1), 1, MAXB).astype(jnp.int32)
    vis_row = place_ends(jax.random.randint(key_of[4], (NSUB, MAXB), 0, SG), jax.random.fold_in(key_of[4], 1), 0, SG - 1).astype(jnp.int32)
    vis_weight = jnp.clip(jax.random.uniform(key_of[5], (NSUB, MAXB, SG), jnp.float32, -1.0, 1.0) * steps_of(key_of[5], (NSUB, MAXB, SG), ((0, 16), (2, 16)), -0.4, 0.0), -1.0, 1.0)
    return {"facets": facets, "column_start": column_start, "subgrid_start": subgrid_start, "vis_count": vis_count, "vis_row": vis_row, "vis_weight": vis_weight}


HIGH = lax.Precision.HIGHEST

def table(first, count, anchor, length, modulus):
    freqs = (first + jnp.arange(count, dtype=jnp.int32)) % modulus
    coords = anchor + jnp.arange(length, dtype=jnp.int32)
    phase = freqs[:, None] * coords[None, :] % modulus
    angle = phase.astype(jnp.float32) * jnp.float32(2.0 * math.pi / modulus)
    scale = jnp.float32(1.0 / math.sqrt(modulus))
    return (jnp.cos(angle) * scale, jnp.sin(angle) * scale)

def contract(form, left, right):
    return jnp.einsum(form, left, right, precision=HIGH)

def reference(facets, column_start, subgrid_start, vis_count, vis_row, vis_weight):
    real_part, imag_part = (facets[0], facets[1])
    col_cos, col_sin = table(column_start[0], SG, 0, N2, N2)
    strip_re = contract('qy,xy->qx', col_cos, real_part) + contract('qy,xy->qx', col_sin, imag_part)
    strip_im = contract('qy,xy->qx', col_cos, imag_part) - contract('qy,xy->qx', col_sin, real_part)

    def forward(first):
        row_cos, row_sin = table(first, SG, 0, N1, N1)
        sub_re = contract('qx,px->qp', strip_re, row_cos) + contract('qx,px->qp', strip_im, row_sin)
        sub_im = contract('qx,px->qp', strip_im, row_cos) - contract('qx,px->qp', strip_re, row_sin)
        return jnp.stack([sub_re, sub_im], 1)
    subs = lax.map(forward, subgrid_start)
    live = (jnp.arange(MAXB, dtype=jnp.int32)[None, :] < vis_count[:, None]).astype(jnp.float32)
    onehot = (vis_row[:, :, None] == jnp.arange(SG, dtype=jnp.int32)[None, None, :]).astype(jnp.float32)
    gain = 1.0 + contract('sbq,sbp->sqp', vis_weight * live[:, :, None], onehot)
    corrected = subs * gain[:, :, None, :]

    def adjoint(carry, items):
        first, grid = items
        row_cos, row_sin = table(first, SG, 0, N1, N1)
        back_re = contract('qp,px->qx', grid[:, 0], row_cos) - contract('qp,px->qx', grid[:, 1], row_sin)
        back_im = contract('qp,px->qx', grid[:, 1], row_cos) + contract('qp,px->qx', grid[:, 0], row_sin)
        return ((carry[0] + back_re, carry[1] + back_im), None)
    start = (jnp.zeros((SG, N1), jnp.float32), jnp.zeros((SG, N1), jnp.float32))
    (back_re, back_im), unused = lax.scan(adjoint, start, (subgrid_start, corrected))
    image_re = contract('qx,qy->xy', back_re, col_cos) - contract('qx,qy->xy', back_im, col_sin)
    image_im = contract('qx,qy->xy', back_im, col_cos) + contract('qx,qy->xy', back_re, col_sin)
    return (corrected, jnp.stack([image_re, image_im]))
```

```python
import math

import jax
import jax.numpy as jnp
from jax import lax
from jax.experimental import pallas as pl
from jax.experimental.pallas import tpu as pltpu
from jax.sharding import PartitionSpec as P

SG = 512
MAXB = 64
NR = 16
NC = 16
N1 = 2048
N2 = 16384
LW = 1024
LH = 128

F32 = jnp.float32
BF16 = jnp.bfloat16
I32 = jnp.int32
MESH = pl.DeviceIdType.MESH


def iota(shape, axis):
    return lax.broadcasted_iota(I32, shape, axis)


def sincos(t, lg):
    q = (t + (1 << (lg - 3))) >> (lg - 2)
    r = t - (q << (lg - 2))
    th = r.astype(F32) * F32(2.0 * math.pi / (1 << lg))
    z = th * th
    s = th * (1.0 + z * (-1.0 / 6 + z * (1.0 / 120 + z * (-1.0 / 5040 + z * (1.0 / 362880)))))
    c = 1.0 + z * (-0.5 + z * (1.0 / 24 + z * (-1.0 / 720 + z * (1.0 / 40320))))
    odd = (q & 1) == 1
    cc = jnp.where(odd, s, c)
    ss = jnp.where(odd, c, s)
    return (
        jnp.where(((q + 1) & 2) != 0, -cc, cc),
        jnp.where((q & 2) != 0, -ss, ss),
    )


def split(x):
    hi = x.astype(BF16)
    return hi, (x - hi.astype(F32)).astype(BF16)


def dot(a, b):
    return lax.dot_general(a, b, (((1,), (0,)), ((), ())), preferred_element_type=F32)


def dot_t(a, b):
    return lax.dot_general(a, b, (((1,), (1,)), ((), ())), preferred_element_type=F32)


def dot3(a, b):
    ah, al = split(a)
    bh, bl = split(b)
    return dot(ah, bh) + (dot(ah, bl) + dot(al, bh))


def kernel(
    cs_ref, ss_ref, vc_ref, vr_ref, vw_ref, fac_hbm,
    cor_hbm, img_hbm,
    xv, rh, rl, arow, thi, tlo, part,
    rec_k, snd_h, rec_h, snd_y, rec_y,
    snd_a, rec_a, d1, twc, tws, gai_s, gai_r, g_s, g_r,
    snd_b, rec_b, agb, cor_v, img_v,
    load_sem, out_sem, ks_sem, kr_sem, hs_sem, hr_sem, ys_sem, yr_sem,
    gs_sem, gr_sem, as_sem, ar_sem, cs_sem, cr_sem, bs_sem, br_sem,
    ays_sem, ayr_sem, ahs_sem, ahr_sem, aks_sem, akr_sem,
):
    r = lax.axis_index("frow")
    c = lax.axis_index("fcol")
    y = c // 4
    h = (c // 2) % 2
    k = c % 2
    dev_k = (r, c + 1 - 2 * k)
    dev_h = (r, c + 2 - 4 * h)
    y_peers = [(y + d) % 4 for d in range(4)]
    dev_y = [(r, yp * 4 + c % 4) for yp in y_peers]
    r_peers = [(r + d) % NR for d in range(NR)]
    dev_r = [(rp, c) for rp in r_peers]

    def remote(src, dst, ssem, rsem, dev):
        return pltpu.make_async_remote_copy(
            src_ref=src, dst_ref=dst, send_sem=ssem, recv_sem=rsem,
            device_id=dev, device_id_type=MESH,
        )

    barrier = pltpu.get_barrier_semaphore()
    for dev in [dev_k, dev_h] + dev_y[1:] + dev_r[1:]:
        pl.semaphore_signal(barrier, inc=1, device_id=dev, device_id_type=MESH)

    load = pltpu.make_async_copy(fac_hbm, xv, load_sem)
    load.start()

    f = cs_ref[0]
    off = c * LW
    coord = off + iota((32, LW), 1)
    g = iota((32, LW), 0)
    qbase = ((g >> 1) & 3) * 128 + ((g >> 3) & 1) * 64 + (g >> 4) * 32 + (g & 1) * 16
    t = (((f + qbase) & (N2 - 1)) * coord) & (N2 - 1)
    ac, asn = sincos(t, 14)
    arow[0] = ac * F32(1.0 / math.sqrt(N2))
    arow[1] = asn * F32(1.0 / math.sqrt(N2))
    bc, bs = sincos((iota((16, LW), 0) * (off + iota((16, LW), 1))) & (N2 - 1), 14)

    @pl.loop(0, 32)
    def _(i):
        ca = arow[0, pl.ds(i, 1), :]
        sa = arow[1, pl.ds(i, 1), :]
        rows = pl.ds(pl.multiple_of(i * 16, 16), 16)
        th, tl = split(ca * bc - sa * bs)
        thi[0, rows, :] = th
        tlo[0, rows, :] = tl
        th, tl = split(sa * bc + ca * bs)
        thi[1, rows, :] = th
        tlo[1, rows, :] = tl

    load.wait()
    xr = xv[0]
    xi = xv[1]
    xrh, xrl = split(xr)
    xih, xil = split(xi)
    rh[0, 0:LH] = xrh
    rh[0, LH:] = xih
    rh[1, 0:LH] = xih
    rh[1, LH:] = -xrh
    rl[0, 0:LH] = xrl
    rl[0, LH:] = xil
    rl[1, 0:LH] = xil
    rl[1, LH:] = -xrl

    def strip_half(kk):
        rows = pl.ds(pl.multiple_of(kk * 256, 256), 256)
        acc = None
        for m in range(2):
            a = thi[m, rows, :]
            b = tlo[m, rows, :]
            s = dot_t(a, rh[m]) + (dot_t(a, rl[m]) + dot_t(b, rh[m]))
            acc = s if acc is None else acc + s
        for hh in range(2):
            for yy in range(4):
                base = (hh * 4 + yy) * 32
                for p in range(2):
                    part[kk, hh, yy, p] = acc[base : base + 32, p * LH : (p + 1) * LH]

    strip_half(1 - k)
    pl.semaphore_wait(barrier, 20)
    k_copy = remote(part.at[1 - k], rec_k, ks_sem, kr_sem, dev_k)
    k_copy.start()
    strip_half(k)

    rows_l = vr_ref[...]
    diag = iota((MAXB, MAXB), 0) == iota((MAXB, MAXB), 1)
    row_c = jnp.sum(
        jnp.where(diag, jnp.broadcast_to(rows_l, (MAXB, MAXB)).astype(F32), 0.0), axis=1, keepdims=True
    )
    row_c = row_c.astype(I32)
    wide = NR * 128
    lane = iota((32, wide), 1)
    sel = (iota((32, wide), 0) == ((lane >> 6) & 1) * 16 + (lane >> 7)).astype(F32).astype(BF16)
    w = vw_ref[0]
    w1 = w.astype(BF16)
    rest = w - w1.astype(F32)
    w2 = rest.astype(BF16)
    w3 = (rest - w2.astype(F32)).astype(BF16)
    wide_w = (dot(w1, sel) + dot(w2, sel)) + dot(w3, sel)
    wide_w = jnp.where((row_c >> 4) == (iota((MAXB, wide), 1) & 31), wide_w, 0.0)
    wh, wl = split(wide_w)
    low = jnp.broadcast_to(rows_l, (16, MAXB)) & 15
    lhs = ((low == iota((16, MAXB), 0)) & (iota((16, MAXB), 1) < vc_ref[0])).astype(F32).astype(BF16)
    gain = 1.0 + (dot(lhs, wh) + dot(lhs, wl))
    for i in range(NR):
        gai_s[i] = gain[:, i * 128 : (i + 1) * 128]

    k_copy.wait_recv()
    for yy in range(4):
        snd_h[yy] = part[k, 1 - h, yy] + rec_k[1 - h, yy]
    h_copy = remote(snd_h, rec_h, hs_sem, hr_sem, dev_h)
    h_copy.start()
    g_copies = [
        remote(gai_s.at[r_peers[d]], gai_r.at[r], gs_sem.at[d], gr_sem.at[d], dev_r[d])
        for d in range(1, NR)
    ]
    for cp in g_copies:
        cp.start()
    gai_r[r] = gai_s[r]

    mu = iota((16, 128), 0)
    lb = iota((16, 128), 1)

    @pl.loop(0, NR)
    def _(s):
        kf = (ss_ref[s] + mu) & (N1 - 1)
        rows = pl.ds(pl.multiple_of(s * 16, 16), 16)
        cc, sn = sincos((kf * lb) & (N1 - 1), 11)
        twc[rows, :] = cc * F32(1.0 / math.sqrt(N1))
        tws[rows, :] = sn * F32(1.0 / math.sqrt(N1))
        ca, sa = sincos((kf * (lb & 15)) & 15, 4)
        pi = (lb >> 4) & 1
        blk = lb >> 5
        for po in range(2):
            v = jnp.where(pi == 0, ca, sa) if po == 0 else jnp.where(pi == 0, -sa, ca)
            hi = v.astype(BF16).astype(F32)
            v = jnp.where(blk < 2, hi, jnp.where(blk == 2, v - hi, 0.0))
            d1[po, rows, :] = v.astype(BF16)

    row = iota((512, 128), 0)
    col = iota((512, 128), 1)
    cc, sn = sincos(((row & 127) * (col & 31)) & 127, 7)
    pin = (row >> 7) & 1
    pout = (col >> 5) & 1
    same = (row >> 8) == (col >> 6)
    e3 = jnp.where(pin == pout, cc, jnp.where(pin == 1, sn, -sn))
    e3h, e3l = split(jnp.where(same, e3, 0.0))
    row = iota((128, 512), 0)
    col = iota((128, 512), 1)
    cc, sn = sincos(((col & 127) * (row & 31)) & 127, 7)
    pin = (row >> 5) & 1
    pout = (col >> 7) & 1
    same = (col >> 8) == (row >> 6)
    e4 = jnp.where(pin == pout, cc, jnp.where(pin == 1, -sn, sn))
    e4h, e4l = split(jnp.where(same, e4, 0.0))
    lane = iota((16, 256), 1)
    first = jnp.zeros((16, 256), I32)
    for s in range(NR):
        first = jnp.where((lane >> 4) == s, ss_ref[s], first)
    ca, sa = sincos(((first + (lane & 15)) * iota((16, 256), 0)) & 15, 4)
    d2 = jnp.concatenate(
        [jnp.concatenate([ca, -sa], axis=1), jnp.concatenate([sa, ca], axis=1)], axis=0
    )
    d2h, d2l = split(d2)

    h_copy.wait_recv()
    for yy in range(4):
        snd_y[yy] = (part[k, h, yy] + rec_k[h, yy]) + rec_h[yy]
    y_copies = [
        remote(snd_y.at[y_peers[d]], rec_y.at[d - 1], ys_sem.at[d], yr_sem.at[d], dev_y[d])
        for d in range(1, 4)
    ]
    for cp in y_copies:
        cp.start()
    for cp in y_copies:
        cp.wait_recv()
    strip = (snd_y[y] + rec_y[0]) + (rec_y[1] + rec_y[2])
    for p in range(2):
        for q in range(2):
            snd_a[:, p * 2 + q, :] = strip[p, q * 16 : (q + 1) * 16, :]
    a_copies = [
        remote(snd_a.at[r_peers[d]], rec_a.at[r], as_sem.at[d], ar_sem.at[d], dev_r[d])
        for d in range(1, NR)
    ]
    for cp in a_copies:
        cp.start()
    rec_a[r] = snd_a[r]
    for cp in a_copies:
        cp.wait_recv()
    for cp in g_copies:
        cp.wait_recv()

    v = jnp.concatenate(
        [jnp.concatenate([rec_a[:, p * 2 + q, :] for q in range(2)], axis=1) for p in range(2)], axis=0
    )
    vh, vl = split(v)
    stack = jnp.concatenate([vh, vl, vh, jnp.zeros_like(vh)], axis=0)
    zre = dot(d1[0], stack)
    zim = dot(d1[1], stack)
    tc = twc[...]
    ts = tws[...]
    cols = []
    for q in range(2):
        re = zre[:, q * 128 : (q + 1) * 128]
        im = zim[:, q * 128 : (q + 1) * 128]
        cols += [re * tc + im * ts, im * tc - re * ts]
    zh, zl = split(jnp.concatenate(cols, axis=1))
    sub = dot(zh, e3h) + (dot(zh, e3l) + dot(zl, e3h))
    grid = sub * gai_r[...].reshape(256, 128)
    g_s[...] = grid.reshape(NR, 16, 128)
    c_copies = [
        remote(g_s.at[r_peers[d]], g_r.at[r], cs_sem.at[d], cr_sem.at[d], dev_r[d])
        for d in range(1, NR)
    ]
    for cp in c_copies:
        cp.start()
    gh, gl = split(grid)
    vv = dot(gh, e4h) + (dot(gh, e4l) + dot(gl, e4h))
    res = []
    ims = []
    for q in range(2):
        re = vv[:, q * 256 : q * 256 + 128]
        im = vv[:, q * 256 + 128 : q * 256 + 256]
        res.append(re * tc - im * ts)
        ims.append(im * tc + re * ts)
    both = jnp.concatenate([jnp.concatenate(res, axis=1), jnp.concatenate(ims, axis=1)], axis=0)
    bh, bl = split(both)
    back = dot(d2h, bh) + (dot(d2h, bl) + dot(d2l, bh))
    for p in range(2):
        for q in range(2):
            snd_b[:, p * 2 + q, :] = back[p * 16 : (p + 1) * 16, q * 128 : (q + 1) * 128]
    b_copies = [
        remote(snd_b.at[r_peers[d]], rec_b.at[r], bs_sem.at[d], br_sem.at[d], dev_r[d])
        for d in range(1, NR)
    ]
    for cp in b_copies:
        cp.start()
    rec_b[r] = snd_b[r]
    g_r[r] = g_s[r]
    for cp in b_copies:
        cp.wait_recv()
    for p in range(2):
        for q in range(2):
            agb[k, h, y, p, q * 16 : (q + 1) * 16, :] = rec_b[:, p * 2 + q, :]

    mine = agb.at[k, h, y]
    ay = [
        remote(mine, mine, ays_sem.at[d], ayr_sem.at[d], dev_y[d]) for d in range(1, 4)
    ]
    from_y = [agb.at[k, h, (y + 4 - d) % 4] for d in range(4)]
    ah = [remote(from_y[d], from_y[d], ahs_sem.at[d], ahr_sem.at[d], dev_h) for d in range(4)]
    ak = [remote(from_y[d], from_y[d], aks_sem.at[d], akr_sem.at[d], dev_k) for d in range(4)]
    oth = agb.at[k, 1 - h]
    ak_h = remote(oth, oth, aks_sem.at[4], akr_sem.at[4], dev_k)
    for cp in ay:
        cp.start()
    ah[0].start()
    ak[0].start()
    for d in range(1, 4):
        in_y = remote(from_y[d], from_y[d], ays_sem.at[d], ayr_sem.at[d], dev_y[d])
        in_y.wait_recv()
        ah[d].start()
        ak[d].start()

    for cp in c_copies:
        cp.wait_recv()
    lane = iota((128, SG), 1)
    rowi = iota((128, SG), 0)
    gath = g_r[...].reshape(256, 128)
    g1 = gath.astype(BF16)
    rest = gath - g1.astype(F32)
    g2 = rest.astype(BF16)
    g3 = (rest - g2.astype(F32)).astype(BF16)
    keep = (iota((256, SG), 0) & 15) == (iota((256, SG), 1) & 15)
    for q in range(2):
        for p in range(2):
            ex = (rowi == (q * 2 + p) * 32 + (lane >> 4)).astype(F32).astype(BF16)
            wide_g = (dot(g1, ex) + dot(g2, ex)) + dot(g3, ex)
            wide_g = jnp.where(keep, wide_g, 0.0)
            cor_v[0, q * 16 : (q + 1) * 16, p, :] = jnp.sum(wide_g.reshape(16, 16, SG), axis=1)
    cor_out = pltpu.make_async_copy(cor_v, cor_hbm, out_sem.at[4])
    cor_out.start()

    for d in range(4):
        src = agb.at[k, 1 - h, (y + 4 - d) % 4]
        remote(src, src, ahs_sem.at[d], ahr_sem.at[d], dev_h).wait_recv()
    ak_h.start()
    for d in range(4):
        src = agb.at[1 - k, h, (y + 4 - d) % 4]
        remote(src, src, aks_sem.at[d], akr_sem.at[d], dev_k).wait_recv()
    src = agb.at[1 - k, 1 - h]
    remote(src, src, aks_sem.at[4], akr_sem.at[4], dev_k).wait_recv()

    bre = []
    bim = []
    for kk in range(2):
        for hh in range(2):
            for yy in range(4):
                bre.append(agb[kk, hh, yy, 0])
                bim.append(agb[kk, hh, yy, 1])
    re_t = jnp.concatenate(bre, axis=0).T
    im_t = jnp.concatenate(bim, axis=0).T
    l1h, l1l = split(jnp.concatenate([re_t, im_t], axis=0))
    l2h, l2l = split(jnp.concatenate([-im_t, re_t], axis=0))
    outs = []
    for n in range(4):
        cols = slice(n * 256, (n + 1) * 256)
        ch = thi[0, :, cols]
        cl = tlo[0, :, cols]
        sh = thi[1, :, cols]
        sl = tlo[1, :, cols]
        o = (dot(l1h, ch) + dot(l2h, sh)) + (
            (dot(l1l, ch) + dot(l2l, sh)) + (dot(l1h, cl) + dot(l2h, sl))
        )
        img_v[0, :, cols] = o[:LH]
        img_v[1, :, cols] = o[LH:]
        cp = pltpu.make_async_copy(img_v.at[:, :, cols], img_hbm.at[:, :, cols], out_sem.at[n])
        cp.start()
        outs.append(cp)

    for cp in [k_copy, h_copy, *y_copies, *g_copies, *a_copies, *c_copies, *b_copies, *ay, *ah, *ak, ak_h]:
        cp.wait_send()
    for cp in outs:
        cp.wait()
    cor_out.wait()


def per_device(facets, column_start, subgrid_start, vis_count, vis_row, vis_weight):
    dma = pltpu.SemaphoreType.DMA
    vm = pltpu.VMEM
    smem = pl.BlockSpec(memory_space=pltpu.SMEM)
    vmem = pl.BlockSpec(memory_space=pltpu.VMEM)
    anym = pl.BlockSpec(memory_space=pl.ANY)
    return pl.pallas_call(
        kernel,
        out_shape=(
            jax.ShapeDtypeStruct((1, 32, 2, SG), F32),
            jax.ShapeDtypeStruct((2, LH, LW), F32),
        ),
        in_specs=[smem, smem, smem, vmem, vmem, anym],
        out_specs=(anym, anym),
        scratch_shapes=[
            vm((2, LH, LW), F32),
            vm((2, 2 * LH, LW), BF16),
            vm((2, 2 * LH, LW), BF16),
            vm((2, 32, LW), F32),
            vm((2, SG, LW), BF16),
            vm((2, SG, LW), BF16),
            vm((2, 2, 4, 2, 32, LH), F32),
            vm((2, 4, 2, 32, LH), F32),
            vm((4, 2, 32, LH), F32),
            vm((4, 2, 32, LH), F32),
            vm((4, 2, 32, LH), F32),
            vm((3, 2, 32, LH), F32),
            vm((NR, 4, 128), F32),
            vm((NR, 4, 128), F32),
            vm((2, 256, 128), BF16),
            vm((256, 128), F32),
            vm((256, 128), F32),
            vm((NR, 16, 128), F32),
            vm((NR, 16, 128), F32),
            vm((NR, 16, 128), F32),
            vm((NR, 16, 128), F32),
            vm((NR, 4, 128), F32),
            vm((NR, 4, 128), F32),
            vm((2, 2, 4, 2, 32, LH), F32),
            vm((1, 32, 2, SG), F32),
            vm((2, LH, LW), F32),
            dma, dma((5,)), dma, dma, dma, dma, dma((4,)), dma((4,)),
            dma((NR,)), dma((NR,)), dma((NR,)), dma((NR,)), dma((NR,)), dma((NR,)), dma((NR,)), dma((NR,)),
            dma((4,)), dma((4,)), dma((4,)), dma((4,)), dma((5,)), dma((5,)),
        ],
        compiler_params=pltpu.CompilerParams(collective_id=0, has_side_effects=True),
    )(column_start, subgrid_start, vis_count, vis_row, vis_weight, facets)


def solution(mesh):
    return jax.shard_map(
        per_device,
        mesh=mesh,
        in_specs=(
            P(None, "frow", "fcol"),
            P(),
            P(),
            P("frow"),
            P("frow", None),
            P("frow", None, "fcol"),
        ),
        out_specs=(P("frow", "fcol", None, None), P(None, "frow", "fcol")),
        check_vma=False,
    )
```

```python
import math

import jax
import jax.numpy as jnp
from jax import lax
from jax.experimental import pallas as pl
from jax.experimental.pallas import tpu as pltpu
from jax.sharding import PartitionSpec as P

SG = 512
MAXB = 64
NR = 16
NC = 16
N1 = 2048
N2 = 16384
LW = 1024
LH = 128

F32 = jnp.float32
BF16 = jnp.bfloat16
I32 = jnp.int32
MESH = pl.DeviceIdType.MESH


def iota(shape, axis):
    return lax.broadcasted_iota(I32, shape, axis)


def sincos(t, lg):
    q = (t + (1 << (lg - 3))) >> (lg - 2)
    r = t - (q << (lg - 2))
    th = r.astype(F32) * F32(2.0 * math.pi / (1 << lg))
    z = th * th
    s = th * (1.0 + z * (-1.0 / 6 + z * (1.0 / 120 + z * (-1.0 / 5040 + z * (1.0 / 362880)))))
    c = 1.0 + z * (-0.5 + z * (1.0 / 24 + z * (-1.0 / 720 + z * (1.0 / 40320))))
    odd = (q & 1) == 1
    cc = jnp.where(odd, s, c)
    ss = jnp.where(odd, c, s)
    return (
        jnp.where(((q + 1) & 2) != 0, -cc, cc),
        jnp.where((q & 2) != 0, -ss, ss),
    )


def split(x):
    hi = x.astype(BF16)
    return hi, (x - hi.astype(F32)).astype(BF16)


def dot(a, b):
    return lax.dot_general(a, b, (((1,), (0,)), ((), ())), preferred_element_type=F32)


def dot_t(a, b):
    return lax.dot_general(a, b, (((1,), (1,)), ((), ())), preferred_element_type=F32)


def dot3(a, b):
    ah, al = split(a)
    bh, bl = split(b)
    return dot(ah, bh) + (dot(ah, bl) + dot(al, bh))


def kernel(
    cs_ref, ss_ref, vc_ref, vr_ref, vw_ref, fac_hbm,
    cor_hbm, img_hbm,
    xv, rhi, rlo, tabh, tabl, phase, part, rec_k, snd_y, rec_y,
    snd_a, rec_a, d1, twc, tws, gai_s, gai_r, g_s, g_r,
    snd_b, rec_b, agb, cor_v, img_v,
    load_sem, out_sem, ks_sem, kr_sem, ys_sem, yr_sem,
    gs_sem, gr_sem, as_sem, ar_sem, cs_sem, cr_sem, bs_sem, br_sem,
    ags_sem, agr_sem, fws_sem, fwr_sem,
):
    r = lax.axis_index("frow")
    c = lax.axis_index("fcol")
    y = c // 4
    h = (c // 2) % 2
    k = c % 2
    low_y = 1 - y // 2
    dev_k = (r, c + 1 - 2 * k)
    y_of = [y, 3 - y, (y + 2) % 4, (5 - y) % 4]
    h_of = [h, 1 - h]
    near = [(0, 1), (1, 0), (1, 1)]
    far = [(2, 0), (3, 0), (2, 1), (3, 1)]
    rels = near + far

    def dev_yh(rel):
        return (r, y_of[rel[0]] * 4 + h_of[rel[1]] * 2 + k)

    def group(rel):
        return rel[0] // 2

    r_peers = [(r + d) % NR for d in range(NR)]
    dev_r = [(rp, c) for rp in r_peers]

    def remote(src, dst, ssem, rsem, dev):
        return pltpu.make_async_remote_copy(
            src_ref=src, dst_ref=dst, send_sem=ssem, recv_sem=rsem,
            device_id=dev, device_id_type=MESH,
        )

    barrier = pltpu.get_barrier_semaphore()
    for dev in [dev_k] + [dev_yh(rel) for rel in rels] + dev_r[1:]:
        pl.semaphore_signal(barrier, inc=1, device_id=dev, device_id_type=MESH)

    load = pltpu.make_async_copy(fac_hbm, xv, load_sem)
    load.start()

    f = cs_ref[0]
    off = c * LW
    pair = (y + 1) // 2 % 2
    base_of = [128 * (1 - pair), 128 * pair]
    coord = off + iota((16, LW), 1)
    u = iota((16, LW), 0)
    ibase = jnp.where(u < 8, base_of[0], base_of[1]) + (u & 7) * 16
    ac, asn = sincos(((2 * ibase + 1) * coord) & (2 * N2 - 1), 15)
    bc, bs = sincos((2 * u * coord) & (2 * N2 - 1), 15)
    pc, ps = sincos(((2 * f + SG - 1) * (off + iota((8, LW), 1))) & (2 * N2 - 1), 15)
    pc = pc[0:1] * F32(1.0 / math.sqrt(N2))
    ps = ps[0:1] * F32(1.0 / math.sqrt(N2))
    phase[0:1, :] = pc
    phase[1:2, :] = ps

    def table_group(g):
        for n in range(8):
            ca = ac[g * 8 + n : g * 8 + n + 1]
            sa = asn[g * 8 + n : g * 8 + n + 1]
            th, tl = split(ca * bc - sa * bs)
            tabh[g, n * 16 : n * 16 + 16, :] = th
            tabl[g, n * 16 : n * 16 + 16, :] = tl
            th, tl = split(sa * bc + ca * bs)
            tabh[g, 128 + n * 16 : 144 + n * 16, :] = th
            tabl[g, 128 + n * 16 : 144 + n * 16, :] = tl

    table_group(1)
    load.wait()
    xr = xv[0]
    xi = xv[1]
    hi, lo = split(xr * pc + xi * ps)
    rhi[0:LH] = hi
    rlo[0:LH] = lo
    hi, lo = split(xi * pc - xr * ps)
    rhi[LH:] = hi
    rlo[LH:] = lo

    def strip_group(g):
        a = tabh[g]
        acc = dot_t(a, rhi[...]) + (dot_t(a, rlo[...]) + dot_t(tabl[g], rhi[...]))
        for hh in range(2):
            for kk in range(2):
                base = (hh * 2 + kk) * 32
                ar = acc[base : base + 32, :LH]
                ai = acc[base : base + 32, LH:]
                br = acc[128 + base : 160 + base, :LH]
                bi = acc[128 + base : 160 + base, LH:]
                part[g, kk, 0, hh, 0] = ar + bi
                part[g, kk, 0, hh, 1] = ai - br
                part[g, 1 - kk, 1, 1 - hh, 0] = ar - bi
                part[g, 1 - kk, 1, 1 - hh, 1] = ai + br

    strip_group(1)
    table_group(0)
    pl.semaphore_wait(barrier, 23)
    k_copies = [
        remote(part.at[g, 1 - k], rec_k.at[g], ks_sem.at[g], kr_sem.at[g], dev_k) for g in range(2)
    ]
    k_copies[1].start()
    strip_group(0)
    k_copies[0].start()

    def send_group(g, group_rels):
        k_copies[g].wait_recv()
        for sg in range(2):
            for hh in range(2):
                snd_y[g, sg, hh] = part[g, k, sg, hh] + rec_k[g, sg, hh]
        copies = [
            remote(
                snd_y.at[g, 1 - y_of[rel[0]] // 2, h_of[rel[1]]],
                rec_y.at[rels.index(rel)], ys_sem.at[g], yr_sem.at[g], dev_yh(rel),
            )
            for rel in group_rels
        ]
        for cp in copies:
            cp.start()

    send_group(1, far)
    send_group(0, near)

    rows_l = vr_ref[...]
    diag = iota((MAXB, MAXB), 0) == iota((MAXB, MAXB), 1)
    row_c = jnp.sum(
        jnp.where(diag, jnp.broadcast_to(rows_l, (MAXB, MAXB)).astype(F32), 0.0), axis=1, keepdims=True
    )
    row_c = row_c.astype(I32)
    wide = NR * 128
    lane = iota((32, wide), 1)
    place = ((lane >> 6) & 1) * 16 + (lane >> 7)
    place = place + low_y * (31 - 2 * place)
    sel = (iota((32, wide), 0) == place).astype(F32).astype(BF16)
    w = vw_ref[0].T
    w1 = w.astype(BF16)
    rest = w - w1.astype(F32)
    w2 = rest.astype(BF16)
    w3 = (rest - w2.astype(F32)).astype(BF16)
    wide_w = (dot(w1, sel) + dot(w2, sel)) + dot(w3, sel)
    wide_w = jnp.where((row_c >> 4) == (iota((MAXB, wide), 1) & 31), wide_w, 0.0)
    wh, wl = split(wide_w)
    low = jnp.broadcast_to(rows_l, (16, MAXB)) & 15
    lhs = ((low == iota((16, MAXB), 0)) & (iota((16, MAXB), 1) < vc_ref[0])).astype(F32).astype(BF16)
    gain = 1.0 + (dot(lhs, wh) + dot(lhs, wl))
    for i in range(NR):
        gai_s[i] = gain[:, i * 128 : (i + 1) * 128]

    def exchange(src, dst, slot, ssem, rsem):
        for d in range(1, NR):
            remote(src.at[r_peers[d]], dst.at[slot], ssem, rsem, dev_r[d]).start()

    def all_of(dst, ssem, rsem):
        some = dst.at[pl.ds(0, NR - 1)]
        return remote(some, some, ssem, rsem, dev_r[1])

    exchange(gai_s, gai_r, r, gs_sem, gr_sem)
    gai_r[r] = gai_s[r]

    mu = iota((16, 128), 0)
    lb = iota((16, 128), 1)

    @pl.loop(0, NR)
    def _(s):
        kf = (ss_ref[s] + mu) & (N1 - 1)
        rows = pl.ds(pl.multiple_of(s * 16, 16), 16)
        cc, sn = sincos((kf * lb) & (N1 - 1), 11)
        twc[rows, :] = cc * F32(1.0 / math.sqrt(N1))
        tws[rows, :] = sn * F32(1.0 / math.sqrt(N1))
        ca, sa = sincos((kf * (lb & 15)) & 15, 4)
        pi = (lb >> 4) & 1
        blk = lb >> 5
        for po in range(2):
            v = jnp.where(pi == 0, ca, sa) if po == 0 else jnp.where(pi == 0, -sa, ca)
            hi = v.astype(BF16).astype(F32)
            v = jnp.where(blk < 2, hi, jnp.where(blk == 2, v - hi, 0.0))
            d1[po, rows, :] = v.astype(BF16)

    row = iota((512, 128), 0)
    col = iota((512, 128), 1)
    cc, sn = sincos(((row & 127) * (col & 31)) & 127, 7)
    pin = (row >> 7) & 1
    pout = (col >> 5) & 1
    same = (row >> 8) == (col >> 6)
    e3 = jnp.where(pin == pout, cc, jnp.where(pin == 1, sn, -sn))
    e3h, e3l = split(jnp.where(same, e3, 0.0))
    row = iota((128, 512), 0)
    col = iota((128, 512), 1)
    cc, sn = sincos(((col & 127) * (row & 31)) & 127, 7)
    pin = (row >> 5) & 1
    pout = (col >> 7) & 1
    same = (col >> 8) == (row >> 6)
    e4 = jnp.where(pin == pout, cc, jnp.where(pin == 1, -sn, sn))
    e4h, e4l = split(jnp.where(same, e4, 0.0))
    lane = iota((16, 256), 1)
    first = jnp.zeros((16, 256), I32)
    for s in range(NR):
        first = jnp.where((lane >> 4) == s, ss_ref[s], first)
    ca, sa = sincos(((first + (lane & 15)) * iota((16, 256), 0)) & 15, 4)
    d2 = jnp.concatenate(
        [jnp.concatenate([ca, -sa], axis=1), jnp.concatenate([sa, ca], axis=1)], axis=0
    )
    d2h, d2l = split(d2)

    far_in = rec_y.at[pl.ds(3, 4)]
    near_in = rec_y.at[pl.ds(0, 3)]
    far_all = remote(far_in, far_in, ys_sem.at[1], yr_sem.at[1], dev_yh(far[0]))
    near_all = remote(near_in, near_in, ys_sem.at[0], yr_sem.at[0], dev_yh(near[0]))
    near_all.wait_recv()
    far_all.wait_recv()
    strip = (
        (snd_y[0, low_y, h] + rec_y[0]) + (rec_y[1] + rec_y[2])
    ) + ((rec_y[3] + rec_y[4]) + (rec_y[5] + rec_y[6]))
    for p in range(2):
        for q in range(2):
            snd_a[:, p * 2 + q, :] = strip[p, q * 16 : (q + 1) * 16, :]
    exchange(snd_a, rec_a, r, as_sem, ar_sem)
    rec_a[r] = snd_a[r]
    all_of(gai_r, gs_sem, gr_sem).wait_recv()
    all_of(rec_a, as_sem, ar_sem).wait_recv()

    v = jnp.concatenate(
        [jnp.concatenate([rec_a[:, p * 2 + q, :] for q in range(2)], axis=1) for p in range(2)], axis=0
    )
    vh, vl = split(v)
    stack = jnp.concatenate([vh, vl, vh, jnp.zeros_like(vh)], axis=0)
    zre = dot(d1[0], stack)
    zim = dot(d1[1], stack)
    tc = twc[...]
    ts = tws[...]
    cols = []
    for q in range(2):
        re = zre[:, q * 128 : (q + 1) * 128]
        im = zim[:, q * 128 : (q + 1) * 128]
        cols += [re * tc + im * ts, im * tc - re * ts]
    zh, zl = split(jnp.concatenate(cols, axis=1))
    sub = dot(zh, e3h) + (dot(zh, e3l) + dot(zl, e3h))
    grid = sub * gai_r[...].reshape(256, 128)
    g_s[...] = grid.reshape(NR, 16, 128)
    gh, gl = split(grid)
    vv = dot(gh, e4h) + (dot(gh, e4l) + dot(gl, e4h))
    res = []
    ims = []
    for q in range(2):
        re = vv[:, q * 256 : q * 256 + 128]
        im = vv[:, q * 256 + 128 : q * 256 + 256]
        res.append(re * tc - im * ts)
        ims.append(im * tc + re * ts)
    both = jnp.concatenate([jnp.concatenate(res, axis=1), jnp.concatenate(ims, axis=1)], axis=0)
    bh, bl = split(both)
    back = dot(d2h, bh) + (dot(d2h, bl) + dot(d2l, bh))
    for p in range(2):
        for q in range(2):
            snd_b[:, p * 2 + q, :] = back[p * 16 : (p + 1) * 16, q * 128 : (q + 1) * 128]
    exchange(snd_b, rec_b, r, bs_sem, br_sem)
    slot = r + low_y * (NR - 1 - 2 * r)
    exchange(g_s, g_r, slot, cs_sem, cr_sem)
    rec_b[r] = snd_b[r]
    g_r[slot] = g_s[r]
    all_of(rec_b, bs_sem, br_sem).wait_recv()
    for p in range(2):
        for q in range(2):
            agb[0, k, low_y, h, p, q * 16 : (q + 1) * 16, :] = rec_b[:, p * 2 + q, :]

    mine = agb.at[0, k, low_y, h]
    sends = [
        remote(mine, agb.at[group(rel), k, low_y, h], ags_sem.at[i], agr_sem.at[i], dev_yh(rel))
        for i, rel in enumerate(rels)
    ]
    for cp in sends[3:] + sends[:3]:
        cp.start()

    def block(rel, kk):
        return agb.at[group(rel), kk, 1 - y_of[rel[0]] // 2, h_of[rel[1]]]

    forwards = [
        remote(block(rel, k), block(rel, k), fws_sem.at[i], fwr_sem.at[i], dev_k)
        for i, rel in enumerate(rels + [(0, 0)])
    ]
    forwards[7].start()

    def arrive(i):
        ref = block(rels[i], k)
        remote(ref, ref, ags_sem.at[i], agr_sem.at[i], dev_yh(rels[i])).wait_recv()
        forwards[i].start()

    def forwarded(i):
        ref = block((rels + [(0, 0)])[i], 1 - k)
        remote(ref, ref, fws_sem.at[i], fwr_sem.at[i], dev_k).wait_recv()

    for i in range(7):
        arrive(i)

    def image_lhs(g):
        er, ei, om, orr = [], [], [], []
        for hh in range(2):
            for kk in range(2):
                up = agb[g, kk, 0, hh]
                dn = agb[g, 1 - kk, 1, 1 - hh]
                er.append(up[0] + dn[0])
                ei.append(up[1] + dn[1])
                om.append(dn[1] - up[1])
                orr.append(up[0] - dn[0])
        t = [jnp.concatenate(x, axis=0).T for x in (er, om, ei, orr)]
        return split(
            jnp.concatenate(
                [jnp.concatenate(t[:2], axis=1), jnp.concatenate(t[2:], axis=1)], axis=0
            )
        )

    for i in (7, 0, 1, 2):
        forwarded(i)
    lh, ll = image_lhs(0)
    for n in range(4):
        cols = slice(n * 256, (n + 1) * 256)
        o = dot(lh, tabh[0, :, cols]) + (dot(ll, tabh[0, :, cols]) + dot(lh, tabl[0, :, cols]))
        img_v[0, :, cols] = o[:LH]
        img_v[1, :, cols] = o[LH:]
    for i in (3, 4, 5, 6):
        forwarded(i)
    lh, ll = image_lhs(1)
    outs = []
    for n in range(4):
        cols = slice(n * 256, (n + 1) * 256)
        o = dot(lh, tabh[1, :, cols]) + (dot(ll, tabh[1, :, cols]) + dot(lh, tabl[1, :, cols]))
        re = img_v[0, :, cols] + o[:LH]
        im = img_v[1, :, cols] + o[LH:]
        pc = phase[0:1, cols]
        ps = phase[1:2, cols]
        img_v[0, :, cols] = re * pc - im * ps
        img_v[1, :, cols] = im * pc + re * ps
        cp = pltpu.make_async_copy(img_v.at[:, :, cols], img_hbm.at[:, :, cols], out_sem.at[n])
        cp.start()
        outs.append(cp)

    all_of(g_r, cs_sem, cr_sem).wait_recv()
    lane = iota((128, SG), 1)
    rowi = iota((128, SG), 0)
    gath = g_r[...].reshape(256, 128)
    g1 = gath.astype(BF16)
    rest = gath - g1.astype(F32)
    g2 = rest.astype(BF16)
    g3 = (rest - g2.astype(F32)).astype(BF16)
    keep = (iota((256, SG), 0) & 15) == (iota((256, SG), 1) & 15)
    for q in range(2):
        qq = q + low_y * (1 - 2 * q)
        for p in range(2):
            ex = (rowi == (q * 2 + p) * 32 + (lane >> 4)).astype(F32).astype(BF16)
            wide_g = (dot(g1, ex) + dot(g2, ex)) + dot(g3, ex)
            wide_g = jnp.where(keep, wide_g, 0.0)
            cor_v[0, pl.ds(qq * 16, 16), p, :] = jnp.sum(wide_g.reshape(16, 16, SG), axis=1)
    cor_out = pltpu.make_async_copy(cor_v, cor_hbm, out_sem.at[4])
    cor_out.start()

    for cp in k_copies + sends + forwards:
        cp.wait_send()
    far_all.wait_send()
    near_all.wait_send()
    all_of(gai_r, gs_sem, gr_sem).wait_send()
    all_of(rec_a, as_sem, ar_sem).wait_send()
    all_of(g_r, cs_sem, cr_sem).wait_send()
    all_of(rec_b, bs_sem, br_sem).wait_send()
    for cp in outs:
        cp.wait()
    cor_out.wait()


def per_device(facets, column_start, subgrid_start, vis_count, vis_row, vis_weight):
    dma = pltpu.SemaphoreType.DMA
    vm = pltpu.VMEM
    smem = pl.BlockSpec(memory_space=pltpu.SMEM)
    vmem = pl.BlockSpec(memory_space=pltpu.VMEM)
    anym = pl.BlockSpec(memory_space=pl.ANY)
    return pl.pallas_call(
        kernel,
        out_shape=(
            jax.ShapeDtypeStruct((1, 32, 2, SG), F32),
            jax.ShapeDtypeStruct((2, LH, LW), F32),
        ),
        in_specs=[smem, smem, smem, vmem, vmem, anym],
        out_specs=(anym, anym),
        scratch_shapes=[
            vm((2, LH, LW), F32),
            vm((2 * LH, LW), BF16),
            vm((2 * LH, LW), BF16),
            vm((2, 256, LW), BF16),
            vm((2, 256, LW), BF16),
            vm((8, LW), F32),
            vm((2, 2, 2, 2, 2, 32, LH), F32),
            vm((2, 2, 2, 2, 32, LH), F32),
            vm((2, 2, 2, 2, 32, LH), F32),
            vm((7, 2, 32, LH), F32),
            vm((NR, 4, 128), F32),
            vm((NR, 4, 128), F32),
            vm((2, 256, 128), BF16),
            vm((256, 128), F32),
            vm((256, 128), F32),
            vm((NR, 16, 128), F32),
            vm((NR, 16, 128), F32),
            vm((NR, 16, 128), F32),
            vm((NR, 16, 128), F32),
            vm((NR, 4, 128), F32),
            vm((NR, 4, 128), F32),
            vm((2, 2, 2, 2, 2, 32, LH), F32),
            vm((1, 32, 2, SG), F32),
            vm((2, LH, LW), F32),
            dma, dma((5,)), dma((2,)), dma((2,)), dma((2,)), dma((2,)),
            dma, dma, dma, dma, dma, dma, dma, dma,
            dma((7,)), dma((7,)), dma((8,)), dma((8,)),
        ],
        compiler_params=pltpu.CompilerParams(collective_id=0, has_side_effects=True),
    )(column_start, subgrid_start, vis_count, vis_row, jnp.transpose(vis_weight, (0, 2, 1)), facets)


def solution(mesh):
    return jax.shard_map(
        per_device,
        mesh=mesh,
        in_specs=(
            P(None, "frow", "fcol"),
            P(),
            P(),
            P("frow"),
            P("frow", None),
            P("frow", None, "fcol"),
        ),
        out_specs=(P("frow", "fcol", None, None), P(None, "frow", "fcol")),
        check_vma=False,
    )
```

```python
import math

import jax
import jax.numpy as jnp
from jax import lax
from jax.experimental import pallas as pl
from jax.experimental.pallas import tpu as pltpu
from jax.sharding import PartitionSpec as P

SG = 512
MAXB = 64
NR = 16
NC = 16
N1 = 2048
N2 = 16384
LW = 1024
LH = 128

F32 = jnp.float32
BF16 = jnp.bfloat16
I32 = jnp.int32
MESH = pl.DeviceIdType.MESH


def iota(shape, axis):
    return lax.broadcasted_iota(I32, shape, axis)


def sincos(t, lg):
    q = (t + (1 << (lg - 3))) >> (lg - 2)
    r = t - (q << (lg - 2))
    th = r.astype(F32) * F32(2.0 * math.pi / (1 << lg))
    z = th * th
    s = th * (1.0 + z * (-1.0 / 6 + z * (1.0 / 120 + z * (-1.0 / 5040 + z * (1.0 / 362880)))))
    c = 1.0 + z * (-0.5 + z * (1.0 / 24 + z * (-1.0 / 720 + z * (1.0 / 40320))))
    odd = (q & 1) == 1
    cc = jnp.where(odd, s, c)
    ss = jnp.where(odd, c, s)
    return (
        jnp.where(((q + 1) & 2) != 0, -cc, cc),
        jnp.where((q & 2) != 0, -ss, ss),
    )


def split(x):
    hi = x.astype(BF16)
    return hi, (x - hi.astype(F32)).astype(BF16)


def dot(a, b):
    return lax.dot_general(a, b, (((1,), (0,)), ((), ())), preferred_element_type=F32)


def dot_t(a, b):
    return lax.dot_general(a, b, (((1,), (1,)), ((), ())), preferred_element_type=F32)


def dot3(a, b):
    ah, al = split(a)
    bh, bl = split(b)
    return dot(ah, bh) + (dot(ah, bl) + dot(al, bh))


def kernel(
    cs_ref, vc_ref, ss_hbm, vr_hbm, vw_hbm, fac_hbm,
    cor_hbm, img_hbm,
    ss_ref, vr_ref, vw_ref,
    xv, rhi, rlo, tabh, tabl, phase, part, rec_k, snd_y, rec_y,
    snd_a, rec_a, d1, twc, tws, gai_s, gai_r, g_s, g_r,
    snd_b, rec_b, agb, cor_v, img_v,
    load_sem, out_sem, ks_sem, kr_sem, ys_sem, yr_sem,
    gs_sem, gr_sem, as_sem, ar_sem, cs_sem, cr_sem, bs_sem, br_sem,
    ags_sem, agr_sem, fws_sem, fwr_sem,
):
    r = lax.axis_index("frow")
    c = lax.axis_index("fcol")
    y = c // 4
    h = (c // 2) % 2
    k = c % 2
    low_y = 1 - y // 2
    dev_k = (r, c + 1 - 2 * k)
    y_of = [y, 3 - y, (y + 2) % 4, (5 - y) % 4]
    h_of = [h, 1 - h]
    near = [(1, 1), (0, 1), (1, 0)]
    far = [(2, 1), (3, 1), (2, 0), (3, 0)]
    rels = near + far

    def dev_yh(rel):
        return (r, y_of[rel[0]] * 4 + h_of[rel[1]] * 2 + k)

    def group(rel):
        return rel[0] // 2

    r_peers = [(r + d) % NR for d in range(NR)]
    dev_r = [(rp, c) for rp in r_peers]

    def remote(src, dst, ssem, rsem, dev):
        return pltpu.make_async_remote_copy(
            src_ref=src, dst_ref=dst, send_sem=ssem, recv_sem=rsem,
            device_id=dev, device_id_type=MESH,
        )

    load = pltpu.make_async_copy(fac_hbm, xv, load_sem.at[0])
    load.start()
    small = [
        pltpu.make_async_copy(a, b, load_sem.at[i + 1])
        for i, (a, b) in enumerate([(vr_hbm, vr_ref), (vw_hbm, vw_ref), (ss_hbm, ss_ref)])
    ]
    for cp in small:
        cp.start()

    barrier = pltpu.get_barrier_semaphore()
    for dev in [dev_k] + [dev_yh(rel) for rel in rels] + dev_r[1:]:
        pl.semaphore_signal(barrier, inc=1, device_id=dev, device_id_type=MESH)

    f = cs_ref[0]
    off = c * LW
    pair = (y + 1) // 2 % 2
    base_of = [128 * (1 - pair), 128 * pair]
    coord = off + iota((16, LW), 1)
    u = iota((16, LW), 0)
    ibase = jnp.where(u < 8, base_of[0], base_of[1]) + (u & 7) * 16
    ac, asn = sincos(((2 * ibase + 1) * coord) & (2 * N2 - 1), 15)
    bc, bs = sincos((2 * u * coord) & (2 * N2 - 1), 15)
    pc, ps = sincos(((2 * f + SG - 1) * (off + iota((8, LW), 1))) & (2 * N2 - 1), 15)
    pc = pc[0:1] * F32(1.0 / math.sqrt(N2))
    ps = ps[0:1] * F32(1.0 / math.sqrt(N2))
    phase[0:1, :] = pc
    phase[1:2, :] = ps

    def table_group(g):
        for n in range(8):
            ca = ac[g * 8 + n : g * 8 + n + 1]
            sa = asn[g * 8 + n : g * 8 + n + 1]
            th, tl = split(ca * bc - sa * bs)
            tabh[g, n * 16 : n * 16 + 16, :] = th
            tabl[g, n * 16 : n * 16 + 16, :] = tl
            th, tl = split(sa * bc + ca * bs)
            tabh[g, 128 + n * 16 : 144 + n * 16, :] = th
            tabl[g, 128 + n * 16 : 144 + n * 16, :] = tl

    table_group(1)
    load.wait()
    xr = xv[0]
    xi = xv[1]
    hi, lo = split(xr * pc + xi * ps)
    rhi[0:LH] = hi
    rlo[0:LH] = lo
    hi, lo = split(xi * pc - xr * ps)
    rhi[LH:] = hi
    rlo[LH:] = lo

    def strip_group(g):
        a = tabh[g]
        acc = dot_t(a, rhi[...]) + (dot_t(a, rlo[...]) + dot_t(tabl[g], rhi[...]))
        for hh in range(2):
            for kk in range(2):
                base = (hh * 2 + kk) * 32
                ar = acc[base : base + 32, :LH]
                ai = acc[base : base + 32, LH:]
                br = acc[128 + base : 160 + base, :LH]
                bi = acc[128 + base : 160 + base, LH:]
                part[g, kk, 0, hh, 0] = ar + bi
                part[g, kk, 0, hh, 1] = ai - br
                part[g, 1 - kk, 1, 1 - hh, 0] = ar - bi
                part[g, 1 - kk, 1, 1 - hh, 1] = ai + br

    strip_group(1)
    table_group(0)
    pl.semaphore_wait(barrier, 23)
    k_copies = [
        remote(part.at[g, 1 - k], rec_k.at[g], ks_sem.at[g], kr_sem.at[g], dev_k) for g in range(2)
    ]
    k_copies[1].start()
    strip_group(0)
    k_copies[0].start()

    def send_group(g, group_rels):
        k_copies[g].wait_recv()
        for sg in range(2):
            for hh in range(2):
                snd_y[g, sg, hh] = part[g, k, sg, hh] + rec_k[g, sg, hh]
        copies = [
            remote(
                snd_y.at[g, 1 - y_of[rel[0]] // 2, h_of[rel[1]]],
                rec_y.at[rels.index(rel)], ys_sem.at[g], yr_sem.at[g], dev_yh(rel),
            )
            for rel in group_rels
        ]
        for cp in copies:
            cp.start()

    send_group(1, far)
    send_group(0, near)

    for cp in small:
        cp.wait()
    rows_l = vr_ref[...]
    diag = iota((MAXB, MAXB), 0) == iota((MAXB, MAXB), 1)
    row_c = jnp.sum(
        jnp.where(diag, jnp.broadcast_to(rows_l, (MAXB, MAXB)).astype(F32), 0.0), axis=1, keepdims=True
    )
    row_c = row_c.astype(I32)
    wide = NR * 128
    lane = iota((32, wide), 1)
    place = ((lane >> 6) & 1) * 16 + (lane >> 7)
    place = place + low_y * (31 - 2 * place)
    sel = (iota((32, wide), 0) == place).astype(F32).astype(BF16)
    w = vw_ref[0].T
    w1 = w.astype(BF16)
    rest = w - w1.astype(F32)
    w2 = rest.astype(BF16)
    w3 = (rest - w2.astype(F32)).astype(BF16)
    wide_w = (dot(w1, sel) + dot(w2, sel)) + dot(w3, sel)
    wide_w = jnp.where((row_c >> 4) == (iota((MAXB, wide), 1) & 31), wide_w, 0.0)
    wh, wl = split(wide_w)
    low = jnp.broadcast_to(rows_l, (16, MAXB)) & 15
    lhs = ((low == iota((16, MAXB), 0)) & (iota((16, MAXB), 1) < vc_ref[0])).astype(F32).astype(BF16)
    gain = 1.0 + (dot(lhs, wh) + dot(lhs, wl))
    for i in range(NR):
        gai_s[i] = gain[:, i * 128 : (i + 1) * 128]

    def exchange(src, dst, slot, ssem, rsem):
        for d in range(1, NR):
            remote(src.at[r_peers[d]], dst.at[slot], ssem, rsem, dev_r[d]).start()

    def all_of(dst, ssem, rsem):
        some = dst.at[pl.ds(0, NR - 1)]
        return remote(some, some, ssem, rsem, dev_r[1])

    exchange(gai_s, gai_r, r, gs_sem, gr_sem)
    gai_r[r] = gai_s[r]

    mu = iota((16, 128), 0)
    lb = iota((16, 128), 1)

    @pl.loop(0, NR)
    def _(s):
        kf = (ss_ref[s] + mu) & (N1 - 1)
        rows = pl.ds(pl.multiple_of(s * 16, 16), 16)
        cc, sn = sincos((kf * lb) & (N1 - 1), 11)
        twc[rows, :] = cc * F32(1.0 / math.sqrt(N1))
        tws[rows, :] = sn * F32(1.0 / math.sqrt(N1))
        ca, sa = sincos((kf * (lb & 15)) & 15, 4)
        pi = (lb >> 4) & 1
        blk = lb >> 5
        for po in range(2):
            v = jnp.where(pi == 0, ca, sa) if po == 0 else jnp.where(pi == 0, -sa, ca)
            hi = v.astype(BF16).astype(F32)
            v = jnp.where(blk < 2, hi, jnp.where(blk == 2, v - hi, 0.0))
            d1[po, rows, :] = v.astype(BF16)

    row = iota((512, 128), 0)
    col = iota((512, 128), 1)
    cc, sn = sincos(((row & 127) * (col & 31)) & 127, 7)
    pin = (row >> 7) & 1
    pout = (col >> 5) & 1
    same = (row >> 8) == (col >> 6)
    e3 = jnp.where(pin == pout, cc, jnp.where(pin == 1, sn, -sn))
    e3h, e3l = split(jnp.where(same, e3, 0.0))
    row = iota((128, 512), 0)
    col = iota((128, 512), 1)
    cc, sn = sincos(((col & 127) * (row & 31)) & 127, 7)
    pin = (row >> 5) & 1
    pout = (col >> 7) & 1
    same = (col >> 8) == (row >> 6)
    e4 = jnp.where(pin == pout, cc, jnp.where(pin == 1, -sn, sn))
    e4h, e4l = split(jnp.where(same, e4, 0.0))
    lane = iota((16, 256), 1)
    first = jnp.zeros((16, 256), I32)
    for s in range(NR):
        first = jnp.where((lane >> 4) == s, ss_ref[s], first)
    ca, sa = sincos(((first + (lane & 15)) * iota((16, 256), 0)) & 15, 4)
    d2 = jnp.concatenate(
        [jnp.concatenate([ca, -sa], axis=1), jnp.concatenate([sa, ca], axis=1)], axis=0
    )
    d2h, d2l = split(d2)

    far_in = rec_y.at[pl.ds(3, 4)]
    near_in = rec_y.at[pl.ds(0, 3)]
    far_all = remote(far_in, far_in, ys_sem.at[1], yr_sem.at[1], dev_yh(far[0]))
    near_all = remote(near_in, near_in, ys_sem.at[0], yr_sem.at[0], dev_yh(near[0]))
    near_all.wait_recv()
    far_all.wait_recv()
    strip = (
        (snd_y[0, low_y, h] + rec_y[0]) + (rec_y[1] + rec_y[2])
    ) + ((rec_y[3] + rec_y[4]) + (rec_y[5] + rec_y[6]))
    for p in range(2):
        for q in range(2):
            snd_a[:, p * 2 + q, :] = strip[p, q * 16 : (q + 1) * 16, :]
    exchange(snd_a, rec_a, r, as_sem, ar_sem)
    rec_a[r] = snd_a[r]
    all_of(gai_r, gs_sem, gr_sem).wait_recv()
    all_of(rec_a, as_sem, ar_sem).wait_recv()

    v = jnp.concatenate(
        [jnp.concatenate([rec_a[:, p * 2 + q, :] for q in range(2)], axis=1) for p in range(2)], axis=0
    )
    vh, vl = split(v)
    stack = jnp.concatenate([vh, vl, vh, jnp.zeros_like(vh)], axis=0)
    zre = dot(d1[0], stack)
    zim = dot(d1[1], stack)
    tc = twc[...]
    ts = tws[...]
    cols = []
    for q in range(2):
        re = zre[:, q * 128 : (q + 1) * 128]
        im = zim[:, q * 128 : (q + 1) * 128]
        cols += [re * tc + im * ts, im * tc - re * ts]
    zh, zl = split(jnp.concatenate(cols, axis=1))
    sub = dot(zh, e3h) + (dot(zh, e3l) + dot(zl, e3h))
    grid = sub * gai_r[...].reshape(256, 128)
    g_s[...] = grid.reshape(NR, 16, 128)
    gh, gl = split(grid)
    vv = dot(gh, e4h) + (dot(gh, e4l) + dot(gl, e4h))
    res = []
    ims = []
    for q in range(2):
        re = vv[:, q * 256 : q * 256 + 128]
        im = vv[:, q * 256 + 128 : q * 256 + 256]
        res.append(re * tc - im * ts)
        ims.append(im * tc + re * ts)
    both = jnp.concatenate([jnp.concatenate(res, axis=1), jnp.concatenate(ims, axis=1)], axis=0)
    bh, bl = split(both)
    back = dot(d2h, bh) + (dot(d2h, bl) + dot(d2l, bh))
    for p in range(2):
        for q in range(2):
            snd_b[:, p * 2 + q, :] = back[p * 16 : (p + 1) * 16, q * 128 : (q + 1) * 128]
    exchange(snd_b, rec_b, r, bs_sem, br_sem)
    slot = r + low_y * (NR - 1 - 2 * r)
    exchange(g_s, g_r, slot, cs_sem, cr_sem)
    rec_b[r] = snd_b[r]
    g_r[slot] = g_s[r]
    all_of(rec_b, bs_sem, br_sem).wait_recv()
    for p in range(2):
        for q in range(2):
            agb[0, k, low_y, h, p, q * 16 : (q + 1) * 16, :] = rec_b[:, p * 2 + q, :]

    mine = agb.at[0, k, low_y, h]
    sends = [
        remote(mine, agb.at[group(rel), k, low_y, h], ags_sem.at[i], agr_sem.at[i], dev_yh(rel))
        for i, rel in enumerate(rels)
    ]
    for cp in sends[3:] + sends[:3]:
        cp.start()

    def block(rel, kk):
        return agb.at[group(rel), kk, 1 - y_of[rel[0]] // 2, h_of[rel[1]]]

    forwards = [
        remote(block(rel, k), block(rel, k), fws_sem.at[i], fwr_sem.at[i], dev_k)
        for i, rel in enumerate(rels + [(0, 0)])
    ]
    forwards[7].start()

    def arrive(i):
        ref = block(rels[i], k)
        remote(ref, ref, ags_sem.at[i], agr_sem.at[i], dev_yh(rels[i])).wait_recv()
        forwards[i].start()

    def forwarded(i):
        ref = block((rels + [(0, 0)])[i], 1 - k)
        remote(ref, ref, fws_sem.at[i], fwr_sem.at[i], dev_k).wait_recv()

    all_of(g_r, cs_sem, cr_sem).wait_recv()
    lane = iota((256, SG), 1)
    rowi = iota((256, SG), 0)
    gath = jnp.concatenate(split(g_r[...].reshape(256, 128)), axis=1)
    keep = (rowi & 15) == (lane & 15)
    for q in range(2):
        qq = q + low_y * (1 - 2 * q)
        for p in range(2):
            ex = ((rowi & 127) == (q * 2 + p) * 32 + (lane >> 4)).astype(F32).astype(BF16)
            wide_g = jnp.where(keep, dot(gath, ex), 0.0)
            cor_v[0, pl.ds(qq * 16, 16), p, :] = jnp.sum(wide_g.reshape(16, 16, SG), axis=1)
    cor_out = pltpu.make_async_copy(cor_v, cor_hbm, out_sem.at[4])
    cor_out.start()

    for i in range(7):
        arrive(i)

    def image_lhs(g):
        er, ei, om, orr = [], [], [], []
        for hh in range(2):
            for kk in range(2):
                up = agb[g, kk, 0, hh]
                dn = agb[g, 1 - kk, 1, 1 - hh]
                er.append(up[0] + dn[0])
                ei.append(up[1] + dn[1])
                om.append(dn[1] - up[1])
                orr.append(up[0] - dn[0])
        t = [jnp.concatenate(x, axis=0).T for x in (er, om, ei, orr)]
        return split(
            jnp.concatenate(
                [jnp.concatenate(t[:2], axis=1), jnp.concatenate(t[2:], axis=1)], axis=0
            )
        )

    for i in (7, 0, 1, 2):
        forwarded(i)
    lh, ll = image_lhs(0)
    for n in range(4):
        cols = slice(n * 256, (n + 1) * 256)
        o = dot(lh, tabh[0, :, cols]) + (dot(ll, tabh[0, :, cols]) + dot(lh, tabl[0, :, cols]))
        img_v[0, :, cols] = o[:LH]
        img_v[1, :, cols] = o[LH:]
    for i in (3, 4, 5, 6):
        forwarded(i)
    lh, ll = image_lhs(1)
    outs = []
    for n in range(4):
        cols = slice(n * 256, (n + 1) * 256)
        o = dot(lh, tabh[1, :, cols]) + (dot(ll, tabh[1, :, cols]) + dot(lh, tabl[1, :, cols]))
        re = img_v[0, :, cols] + o[:LH]
        im = img_v[1, :, cols] + o[LH:]
        pc = phase[0:1, cols]
        ps = phase[1:2, cols]
        img_v[0, :, cols] = re * pc - im * ps
        img_v[1, :, cols] = im * pc + re * ps
        cp = pltpu.make_async_copy(img_v.at[:, :, cols], img_hbm.at[:, :, cols], out_sem.at[n])
        cp.start()
        outs.append(cp)

    for cp in k_copies + sends + forwards:
        cp.wait_send()
    far_all.wait_send()
    near_all.wait_send()
    all_of(gai_r, gs_sem, gr_sem).wait_send()
    all_of(rec_a, as_sem, ar_sem).wait_send()
    all_of(g_r, cs_sem, cr_sem).wait_send()
    all_of(rec_b, bs_sem, br_sem).wait_send()
    for cp in outs:
        cp.wait()
    cor_out.wait()


def emit(cor_in, img_in, cor_out, img_out, sem):
    copies = [
        pltpu.make_async_copy(img_in, img_out, sem.at[0]),
        pltpu.make_async_copy(cor_in, cor_out, sem.at[1]),
    ]
    for cp in copies:
        cp.start()
    for cp in copies:
        cp.wait()


def per_device(facets, column_start, subgrid_start, vis_count, vis_row, vis_weight):
    dma = pltpu.SemaphoreType.DMA
    vm = pltpu.VMEM
    smem = pl.BlockSpec(memory_space=pltpu.SMEM)
    hbm = pl.BlockSpec(memory_space=pltpu.HBM)
    anym = pl.BlockSpec(memory_space=pl.ANY)
    stay = [
        pltpu.with_memory_space_constraint(x, pltpu.HBM)
        for x in (subgrid_start, vis_row, jnp.transpose(vis_weight, (0, 2, 1)), facets)
    ]
    cor, img = pl.pallas_call(
        kernel,
        out_shape=(
            jax.ShapeDtypeStruct((1, 32, 2, SG), F32),
            jax.ShapeDtypeStruct((2, LH, LW), F32),
        ),
        in_specs=[smem, smem, hbm, hbm, hbm, hbm],
        out_specs=(anym, anym),
        scratch_shapes=[
            pltpu.SMEM((NR,), I32),
            vm((1, MAXB), I32),
            vm((1, 32, MAXB), F32),
            vm((2, LH, LW), F32),
            vm((2 * LH, LW), BF16),
            vm((2 * LH, LW), BF16),
            vm((2, 256, LW), BF16),
            vm((2, 256, LW), BF16),
            vm((8, LW), F32),
            vm((2, 2, 2, 2, 2, 32, LH), F32),
            vm((2, 2, 2, 2, 32, LH), F32),
            vm((2, 2, 2, 2, 32, LH), F32),
            vm((7, 2, 32, LH), F32),
            vm((NR, 4, 128), F32),
            vm((NR, 4, 128), F32),
            vm((2, 256, 128), BF16),
            vm((256, 128), F32),
            vm((256, 128), F32),
            vm((NR, 16, 128), F32),
            vm((NR, 16, 128), F32),
            vm((NR, 16, 128), F32),
            vm((NR, 16, 128), F32),
            vm((NR, 4, 128), F32),
            vm((NR, 4, 128), F32),
            vm((2, 2, 2, 2, 2, 32, LH), F32),
            vm((1, 32, 2, SG), F32),
            vm((2, LH, LW), F32),
            dma((4,)), dma((5,)), dma((2,)), dma((2,)), dma((2,)), dma((2,)),
            dma, dma, dma, dma, dma, dma, dma, dma,
            dma((7,)), dma((7,)), dma((8,)), dma((8,)),
        ],
        compiler_params=pltpu.CompilerParams(collective_id=0, has_side_effects=True, vmem_limit_bytes=16 * 1024 * 1024),
    )(column_start, vis_count, *stay)
    return pl.pallas_call(
        emit,
        out_shape=(
            jax.ShapeDtypeStruct((1, 32, 2, SG), F32),
            jax.ShapeDtypeStruct((2, LH, LW), F32),
        ),
        in_specs=[anym, anym],
        out_specs=(hbm, hbm),
        scratch_shapes=[dma((2,))],
        compiler_params=pltpu.CompilerParams(vmem_limit_bytes=4 * 1024 * 1024),
    )(cor, img)


def solution(mesh):
    return jax.shard_map(
        per_device,
        mesh=mesh,
        in_specs=(
            P(None, "frow", "fcol"),
            P(),
            P(),
            P("frow"),
            P("frow", None),
            P("frow", None, "fcol"),
        ),
        out_specs=(P("frow", "fcol", None, None), P(None, "frow", "fcol")),
        check_vma=False,
    )
```

```python
import math

import jax
import jax.numpy as jnp
from jax import lax
from jax.experimental import pallas as pl
from jax.experimental.pallas import tpu as pltpu
from jax.sharding import PartitionSpec as P

SG = 512
MAXB = 64
NR = 16
NC = 16
N1 = 2048
N2 = 16384
LW = 1024
LH = 128

F32 = jnp.float32
BF16 = jnp.bfloat16
I32 = jnp.int32
MESH = pl.DeviceIdType.MESH


def iota(shape, axis):
    return lax.broadcasted_iota(I32, shape, axis)


def sincos(t, lg):
    q = (t + (1 << (lg - 3))) >> (lg - 2)
    r = t - (q << (lg - 2))
    th = r.astype(F32) * F32(2.0 * math.pi / (1 << lg))
    z = th * th
    s = th * (1.0 + z * (-1.0 / 6 + z * (1.0 / 120 + z * (-1.0 / 5040 + z * (1.0 / 362880)))))
    c = 1.0 + z * (-0.5 + z * (1.0 / 24 + z * (-1.0 / 720 + z * (1.0 / 40320))))
    odd = (q & 1) == 1
    cc = jnp.where(odd, s, c)
    ss = jnp.where(odd, c, s)
    return (
        jnp.where(((q + 1) & 2) != 0, -cc, cc),
        jnp.where((q & 2) != 0, -ss, ss),
    )


def split(x):
    hi = x.astype(BF16)
    return hi, (x - hi.astype(F32)).astype(BF16)


def dot(a, b):
    return lax.dot_general(a, b, (((1,), (0,)), ((), ())), preferred_element_type=F32)


def dot_t(a, b):
    return lax.dot_general(a, b, (((1,), (1,)), ((), ())), preferred_element_type=F32)


def dot3(a, bh, bl):
    n = a.shape[0]
    ah, al = split(a)
    both = dot(jnp.concatenate([ah, al], axis=0), bh)
    return both[:n] + (dot(ah, bl) + both[n:])


def kernel(
    cs_ref, vc_ref, ss_hbm, vr_hbm, vw_hbm, fac_hbm,
    cor_v, img_v, lhs_v, farh, farl, phase,
    ss_ref, vr_ref, vw_ref,
    xv, tabh, tabl, part, rec_k, snd_y, rec_y,
    snd_a, rec_a, d1, twc, tws, gai_s, gai_r, g_s, g_r,
    snd_b, rec_b, agb,
    load_sem, ks_sem, kr_sem, ys_sem, yr_sem,
    gs_sem, gr_sem, as_sem, ar_sem, cs_sem, cr_sem, bs_sem, br_sem,
    ags_sem, agr_sem, fws_sem, fwr_sem,
):
    r = lax.axis_index("frow")
    c = lax.axis_index("fcol")
    y = c // 4
    h = (c // 2) % 2
    k = c % 2
    low_y = 1 - y // 2
    dev_k = (r, c + 1 - 2 * k)
    y_of = [y, 3 - y, (y + 2) % 4, (5 - y) % 4]
    h_of = [h, 1 - h]
    near = [(1, 1), (0, 1), (1, 0)]
    far = [(2, 1), (3, 1), (2, 0), (3, 0)]
    rels = near + far

    def dev_yh(rel):
        return (r, y_of[rel[0]] * 4 + h_of[rel[1]] * 2 + k)

    def group(rel):
        return rel[0] // 2

    r_peers = [(r + d) % NR for d in range(NR)]
    dev_r = [(rp, c) for rp in r_peers]
    by_distance = sorted(range(1, NR), key=lambda d: abs(d - NR // 2))

    def remote(src, dst, ssem, rsem, dev):
        return pltpu.make_async_remote_copy(
            src_ref=src, dst_ref=dst, send_sem=ssem, recv_sem=rsem,
            device_id=dev, device_id_type=MESH,
        )

    load = pltpu.make_async_copy(fac_hbm, xv, load_sem.at[0])
    load.start()
    small = [
        pltpu.make_async_copy(a, b, load_sem.at[i + 1])
        for i, (a, b) in enumerate([(vr_hbm, vr_ref), (vw_hbm, vw_ref), (ss_hbm, ss_ref)])
    ]
    for cp in small:
        cp.start()

    barrier = pltpu.get_barrier_semaphore()
    for dev in [dev_r[d] for d in by_distance] + [dev_yh(rel) for rel in far + near] + [dev_k]:
        pl.semaphore_signal(barrier, inc=1, device_id=dev, device_id_type=MESH)

    f = cs_ref[0]
    off = c * LW
    pair = (y + 1) // 2 % 2
    base_of = [128 * (1 - pair), 128 * pair]
    u = iota((16, 128), 0)
    place = off + iota((16, 128), 1)
    ibase = jnp.where(u < 8, base_of[0], base_of[1]) + (u & 7) * 16
    turns = [2 * ibase + 1, 2 * u, jnp.full((16, 128), 2 * f + SG - 1, I32)]
    now = [sincos((n * place) & (2 * N2 - 1), 15) for n in turns]
    step = [sincos((n * 128) & (2 * N2 - 1), 15) for n in turns]

    def table_tile(g, a, b):
        tiles = []
        for n in range(8):
            ca = a[0][g * 8 + n : g * 8 + n + 1]
            sa = a[1][g * 8 + n : g * 8 + n + 1]
            tiles.append(split(ca * b[0] - sa * b[1]) + split(sa * b[0] + ca * b[1]))
        return [
            jnp.concatenate([t[e] for t in tiles] + [t[e + 2] for t in tiles], axis=0)
            for e in range(2)
        ]

    columns = [[], []]
    waves = []
    for n in range(8):
        for g in range(2):
            columns[g].append(table_tile(g, now[0], now[1]))
        waves.append([w[0:1] * F32(1.0 / math.sqrt(N2)) for w in now[2]])
        now = [
            (ca * cb - sa * sb, sa * cb + ca * sb) for (ca, sa), (cb, sb) in zip(now, step)
        ]
    tables = [
        [jnp.concatenate([t[e] for t in columns[g]], axis=1) for e in range(2)] for g in range(2)
    ]

    load.wait()
    parts = []
    for n in range(8):
        cols = slice(n * 128, n * 128 + 128)
        pc, ps = waves[n]
        phase[0:1, cols] = pc
        phase[1:2, cols] = ps
        tiles = [[], []]
        for i in range(8):
            rows = slice(i * 16, i * 16 + 16)
            xr = xv[0, rows, cols]
            xi = xv[1, rows, cols]
            tiles[0].append(split(xr * pc + xi * ps))
            tiles[1].append(split(xi * pc - xr * ps))
        parts.append(
            [jnp.concatenate([t[e] for t in tiles[0] + tiles[1]], axis=0) for e in range(2)]
        )
    rhi, rlo = [jnp.concatenate([t[e] for t in parts], axis=1) for e in range(2)]

    def strip_group(g):
        th, tl = tables[g]
        both = dot_t(jnp.concatenate([th, tl], axis=0), rhi)
        acc = both[:256] + (dot_t(th, rlo) + both[256:])
        for hh in range(2):
            for kk in range(2):
                base = (hh * 2 + kk) * 32
                ar = acc[base : base + 32, :LH]
                ai = acc[base : base + 32, LH:]
                br = acc[128 + base : 160 + base, :LH]
                bi = acc[128 + base : 160 + base, LH:]
                part[g, kk, 0, hh, 0] = ar + bi
                part[g, kk, 0, hh, 1] = ai - br
                part[g, 1 - kk, 1, 1 - hh, 0] = ar - bi
                part[g, 1 - kk, 1, 1 - hh, 1] = ai + br

    strip_group(1)
    pl.semaphore_wait(barrier, 23)
    k_copies = [
        remote(part.at[g, 1 - k], rec_k.at[g], ks_sem.at[g], kr_sem.at[g], dev_k) for g in range(2)
    ]
    k_copies[1].start()
    strip_group(0)
    k_copies[0].start()

    def send_group(g, group_rels):
        k_copies[g].wait_recv()
        for sg in range(2):
            for hh in range(2):
                snd_y[g, sg, hh] = part[g, k, sg, hh] + rec_k[g, sg, hh]
        copies = [
            remote(
                snd_y.at[g, 1 - y_of[rel[0]] // 2, h_of[rel[1]]],
                rec_y.at[rels.index(rel)], ys_sem.at[g], yr_sem.at[g], dev_yh(rel),
            )
            for rel in group_rels
        ]
        for cp in copies:
            cp.start()

    send_group(1, far)
    send_group(0, near)

    for cp in small:
        cp.wait()
    rows_l = vr_ref[...]
    diag = iota((MAXB, MAXB), 0) == iota((MAXB, MAXB), 1)
    row_c = jnp.sum(
        jnp.where(diag, jnp.broadcast_to(rows_l, (MAXB, MAXB)).astype(F32), 0.0), axis=1, keepdims=True
    )
    row_c = row_c.astype(I32)
    wide = NR * 128
    lane = iota((32, wide), 1)
    place = ((lane >> 6) & 1) * 16 + (lane >> 7)
    place = place + low_y * (31 - 2 * place)
    sel = (iota((32, wide), 0) == place).astype(F32).astype(BF16)
    w = vw_ref[0].T
    w1 = w.astype(BF16)
    rest = w - w1.astype(F32)
    w2 = rest.astype(BF16)
    w3 = (rest - w2.astype(F32)).astype(BF16)
    wide_w = (dot(w1, sel) + dot(w2, sel)) + dot(w3, sel)
    wide_w = jnp.where((row_c >> 4) == (iota((MAXB, wide), 1) & 31), wide_w, 0.0)
    wh, wl = split(wide_w)
    low = jnp.broadcast_to(rows_l, (16, MAXB)) & 15
    lhs = ((low == iota((16, MAXB), 0)) & (iota((16, MAXB), 1) < vc_ref[0])).astype(F32).astype(BF16)
    gain = 1.0 + (dot(lhs, wh) + dot(lhs, wl))
    for i in range(NR):
        gai_s[i] = gain[:, i * 128 : (i + 1) * 128]

    def exchange(src, dst, slot, ssem, rsem):
        for d in by_distance:
            remote(src.at[r_peers[d]], dst.at[slot], ssem, rsem, dev_r[d]).start()

    def all_of(dst, ssem, rsem):
        some = dst.at[pl.ds(0, NR - 1)]
        return remote(some, some, ssem, rsem, dev_r[1])

    tabh[...] = tables[0][0]
    tabl[...] = tables[0][1]
    farh[...] = tables[1][0]
    farl[...] = tables[1][1]

    mu = iota((16, 128), 0)
    lb = iota((16, 128), 1)

    @pl.loop(0, NR)
    def _(s):
        kf = (ss_ref[s] + mu) & (N1 - 1)
        rows = pl.ds(pl.multiple_of(s * 16, 16), 16)
        cc, sn = sincos((kf * lb) & (N1 - 1), 11)
        twc[rows, :] = cc * F32(1.0 / math.sqrt(N1))
        tws[rows, :] = sn * F32(1.0 / math.sqrt(N1))
        ca, sa = sincos((kf * (lb & 15)) & 15, 4)
        pi = (lb >> 4) & 1
        blk = lb >> 5
        for po in range(2):
            v = jnp.where(pi == 0, ca, sa) if po == 0 else jnp.where(pi == 0, -sa, ca)
            hi = v.astype(BF16).astype(F32)
            v = jnp.where(blk < 2, hi, jnp.where(blk == 2, v - hi, 0.0))
            d1[po, rows, :] = v.astype(BF16)

    exchange(gai_s, gai_r, r, gs_sem, gr_sem)
    gai_r[r] = gai_s[r]

    row = iota((512, 128), 0)
    col = iota((512, 128), 1)
    cc, sn = sincos(((row & 127) * (col & 31)) & 127, 7)
    pin = (row >> 7) & 1
    pout = (col >> 5) & 1
    same = (row >> 8) == (col >> 6)
    e3 = jnp.where(pin == pout, cc, jnp.where(pin == 1, sn, -sn))
    e3h, e3l = split(jnp.where(same, e3, 0.0))
    row = iota((128, 512), 0)
    col = iota((128, 512), 1)
    cc, sn = sincos(((col & 127) * (row & 31)) & 127, 7)
    pin = (row >> 5) & 1
    pout = (col >> 7) & 1
    same = (col >> 8) == (row >> 6)
    e4 = jnp.where(pin == pout, cc, jnp.where(pin == 1, -sn, sn))
    e4h, e4l = split(jnp.where(same, e4, 0.0))
    lane = iota((16, 256), 1)
    first = jnp.zeros((16, 256), I32)
    for s in range(NR):
        first = jnp.where((lane >> 4) == s, ss_ref[s], first)
    ca, sa = sincos(((first + (lane & 15)) * iota((16, 256), 0)) & 15, 4)
    d2 = jnp.concatenate(
        [jnp.concatenate([ca, -sa], axis=1), jnp.concatenate([sa, ca], axis=1)], axis=0
    )

    far_in = rec_y.at[pl.ds(3, 4)]
    near_in = rec_y.at[pl.ds(0, 3)]
    far_all = remote(far_in, far_in, ys_sem.at[1], yr_sem.at[1], dev_yh(far[0]))
    near_all = remote(near_in, near_in, ys_sem.at[0], yr_sem.at[0], dev_yh(near[0]))
    near_all.wait_recv()
    far_all.wait_recv()
    strip = (
        (snd_y[0, low_y, h] + rec_y[0]) + (rec_y[1] + rec_y[2])
    ) + ((rec_y[3] + rec_y[4]) + (rec_y[5] + rec_y[6]))
    for p in range(2):
        for q in range(2):
            snd_a[:, p * 2 + q, :] = strip[p, q * 16 : (q + 1) * 16, :]
    exchange(snd_a, rec_a, r, as_sem, ar_sem)
    rec_a[r] = snd_a[r]
    all_of(gai_r, gs_sem, gr_sem).wait_recv()
    all_of(rec_a, as_sem, ar_sem).wait_recv()

    v = jnp.concatenate(
        [jnp.concatenate([rec_a[:, p * 2 + q, :] for q in range(2)], axis=1) for p in range(2)], axis=0
    )
    vh, vl = split(v)
    stack = jnp.concatenate([vh, vl, vh, jnp.zeros_like(vh)], axis=0)
    zre = dot(d1[0], stack)
    zim = dot(d1[1], stack)
    tc = twc[...]
    ts = tws[...]
    cols = []
    for q in range(2):
        re = zre[:, q * 128 : (q + 1) * 128]
        im = zim[:, q * 128 : (q + 1) * 128]
        cols += [re * tc + im * ts, im * tc - re * ts]
    sub = dot3(jnp.concatenate(cols, axis=1), e3h, e3l)
    grid = sub * gai_r[...].reshape(256, 128)
    g_s[...] = grid.reshape(NR, 16, 128)
    vv = dot3(grid, e4h, e4l)
    res = []
    ims = []
    for q in range(2):
        re = vv[:, q * 256 : q * 256 + 128]
        im = vv[:, q * 256 + 128 : q * 256 + 256]
        res.append(re * tc - im * ts)
        ims.append(im * tc + re * ts)
    both = jnp.concatenate([jnp.concatenate(res, axis=1), jnp.concatenate(ims, axis=1)], axis=0)
    bh, bl = split(both)
    back = dot3(d2, bh, bl)
    for p in range(2):
        for q in range(2):
            snd_b[:, p * 2 + q, :] = back[p * 16 : (p + 1) * 16, q * 128 : (q + 1) * 128]
    exchange(snd_b, rec_b, r, bs_sem, br_sem)
    slot = r + low_y * (NR - 1 - 2 * r)
    exchange(g_s, g_r, slot, cs_sem, cr_sem)
    rec_b[r] = snd_b[r]
    g_r[slot] = g_s[r]
    all_of(rec_b, bs_sem, br_sem).wait_recv()
    for p in range(2):
        for q in range(2):
            agb[0, k, low_y, h, p, q * 16 : (q + 1) * 16, :] = rec_b[:, p * 2 + q, :]

    mine = agb.at[0, k, low_y, h]
    sends = [
        remote(mine, agb.at[group(rel), k, low_y, h], ags_sem.at[i], agr_sem.at[i], dev_yh(rel))
        for i, rel in enumerate(rels)
    ]
    for cp in sends[3:] + sends[:3]:
        cp.start()

    def block(rel, kk):
        return agb.at[group(rel), kk, 1 - y_of[rel[0]] // 2, h_of[rel[1]]]

    forwards = [
        remote(block(rel, k), block(rel, k), fws_sem.at[i], fwr_sem.at[i], dev_k)
        for i, rel in enumerate(rels + [(0, 0)])
    ]
    forwards[7].start()

    def arrive(i):
        ref = block(rels[i], k)
        remote(ref, ref, ags_sem.at[i], agr_sem.at[i], dev_yh(rels[i])).wait_recv()
        forwards[i].start()

    def forwarded(i):
        ref = block((rels + [(0, 0)])[i], 1 - k)
        remote(ref, ref, fws_sem.at[i], fwr_sem.at[i], dev_k).wait_recv()

    all_of(g_r, cs_sem, cr_sem).wait_recv()
    lane = iota((256, SG), 1)
    rowi = iota((256, SG), 0)
    gath = jnp.concatenate(split(g_r[...].reshape(256, 128)), axis=1)
    keep = (rowi & 15) == (lane & 15)
    for q in range(2):
        qq = q + low_y * (1 - 2 * q)
        for p in range(2):
            ex = ((rowi & 127) == (q * 2 + p) * 32 + (lane >> 4)).astype(F32).astype(BF16)
            wide_g = jnp.where(keep, dot(gath, ex), 0.0)
            cor_v[0, pl.ds(qq * 16, 16), p, :] = jnp.sum(wide_g.reshape(16, 16, SG), axis=1)
    for i in range(7):
        arrive(i)

    def image_lhs(g):
        er, ei, om, orr = [], [], [], []
        for hh in range(2):
            for kk in range(2):
                up = agb[g, kk, 0, hh]
                dn = agb[g, 1 - kk, 1, 1 - hh]
                er.append(up[0] + dn[0])
                ei.append(up[1] + dn[1])
                om.append(dn[1] - up[1])
                orr.append(up[0] - dn[0])
        t = [jnp.concatenate(x, axis=0).T for x in (er, om, ei, orr)]
        return jnp.concatenate(
            [jnp.concatenate(t[:2], axis=1), jnp.concatenate(t[2:], axis=1)], axis=0
        )

    for i in (7, 0, 1, 2):
        forwarded(i)
    lhs_g = image_lhs(0)
    for n in range(4):
        cols = slice(n * 256, (n + 1) * 256)
        o = dot3(lhs_g, tabh[:, cols], tabl[:, cols])
        img_v[0, :, cols] = o[:LH]
        img_v[1, :, cols] = o[LH:]
    for i in (3, 4, 5, 6):
        forwarded(i)
    lhs_v[...] = image_lhs(1)

    for cp in k_copies + sends + forwards:
        cp.wait_send()
    far_all.wait_send()
    near_all.wait_send()
    all_of(gai_r, gs_sem, gr_sem).wait_send()
    all_of(rec_a, as_sem, ar_sem).wait_send()
    all_of(g_r, cs_sem, cr_sem).wait_send()
    all_of(rec_b, bs_sem, br_sem).wait_send()


def emit(cor_v, img_v, lhs_v, farh, farl, phase, cor_hbm, img_hbm, buf, sem):
    copies = [pltpu.make_async_copy(cor_v, cor_hbm, sem.at[4])]
    copies[0].start()
    lhs_g = lhs_v[...]
    for n in range(4):
        cols = slice(n * 256, (n + 1) * 256)
        o = dot3(lhs_g, farh[:, cols], farl[:, cols])
        re = img_v[0, :, cols] + o[:LH]
        im = img_v[1, :, cols] + o[LH:]
        pc = phase[0:1, cols]
        ps = phase[1:2, cols]
        buf[0, :, cols] = re * pc - im * ps
        buf[1, :, cols] = im * pc + re * ps
        cp = pltpu.make_async_copy(buf.at[:, :, cols], img_hbm.at[:, :, cols], sem.at[n])
        cp.start()
        copies.append(cp)
    for cp in copies:
        cp.wait()


def per_device(facets, column_start, subgrid_start, vis_count, vis_row, vis_weight):
    dma = pltpu.SemaphoreType.DMA
    vm = pltpu.VMEM
    smem = pl.BlockSpec(memory_space=pltpu.SMEM)
    hbm = pl.BlockSpec(memory_space=pltpu.HBM)
    vmem = pl.BlockSpec(memory_space=pltpu.VMEM)
    anym = pl.BlockSpec(memory_space=pl.ANY)
    stay = [
        pltpu.with_memory_space_constraint(x, pltpu.HBM)
        for x in (subgrid_start, vis_row, jnp.transpose(vis_weight, (0, 2, 1)), facets)
    ]
    rest = pl.pallas_call(
        kernel,
        out_shape=(
            jax.ShapeDtypeStruct((1, 32, 2, SG), F32),
            jax.ShapeDtypeStruct((2, LH, LW), F32),
            jax.ShapeDtypeStruct((2 * LH, 256), F32),
            jax.ShapeDtypeStruct((256, LW), BF16),
            jax.ShapeDtypeStruct((256, LW), BF16),
            jax.ShapeDtypeStruct((8, LW), F32),
        ),
        in_specs=[smem, smem, hbm, hbm, hbm, hbm],
        out_specs=(vmem,) * 6,
        scratch_shapes=[
            pltpu.SMEM((NR,), I32),
            vm((1, MAXB), I32),
            vm((1, 32, MAXB), F32),
            vm((2, LH, LW), F32),
            vm((256, LW), BF16),
            vm((256, LW), BF16),
            vm((2, 2, 2, 2, 2, 32, LH), F32),
            vm((2, 2, 2, 2, 32, LH), F32),
            vm((2, 2, 2, 2, 32, LH), F32),
            vm((7, 2, 32, LH), F32),
            vm((NR, 4, 128), F32),
            vm((NR, 4, 128), F32),
            vm((2, 256, 128), BF16),
            vm((256, 128), F32),
            vm((256, 128), F32),
            vm((NR, 16, 128), F32),
            vm((NR, 16, 128), F32),
            vm((NR, 16, 128), F32),
            vm((NR, 16, 128), F32),
            vm((NR, 4, 128), F32),
            vm((NR, 4, 128), F32),
            vm((2, 2, 2, 2, 2, 32, LH), F32),
            dma((4,)), dma((2,)), dma((2,)), dma((2,)), dma((2,)),
            dma, dma, dma, dma, dma, dma, dma, dma,
            dma((7,)), dma((7,)), dma((8,)), dma((8,)),
        ],
        compiler_params=pltpu.CompilerParams(collective_id=0, has_side_effects=True, vmem_limit_bytes=16 * 1024 * 1024),
    )(column_start, vis_count, *stay)
    return pl.pallas_call(
        emit,
        out_shape=(
            jax.ShapeDtypeStruct((1, 32, 2, SG), F32),
            jax.ShapeDtypeStruct((2, LH, LW), F32),
        ),
        in_specs=[vmem] * 6,
        out_specs=(hbm, hbm),
        scratch_shapes=[vm((2, LH, LW), F32), dma((5,))],
        compiler_params=pltpu.CompilerParams(vmem_limit_bytes=8 * 1024 * 1024),
    )(*rest)


def solution(mesh):
    return jax.shard_map(
        per_device,
        mesh=mesh,
        in_specs=(
            P(None, "frow", "fcol"),
            P(),
            P(),
            P("frow"),
            P("frow", None),
            P("frow", None, "fcol"),
        ),
        out_specs=(P("frow", "fcol", None, None), P(None, "frow", "fcol")),
        check_vma=False,
    )
```

```python
import math

import jax
import jax.numpy as jnp
from jax import lax
from jax.experimental import pallas as pl
from jax.experimental.pallas import tpu as pltpu
from jax.sharding import PartitionSpec as P

SG = 512
MAXB = 64
NR = 16
NC = 16
N1 = 2048
N2 = 16384
LW = 1024
LH = 128

F32 = jnp.float32
BF16 = jnp.bfloat16
I32 = jnp.int32
MESH = pl.DeviceIdType.MESH


def div(a, b):
    return lax.div(a, jnp.int32(b))


def rem(a, b):
    return lax.rem(a, jnp.int32(b))


def iota(shape, axis):
    return lax.broadcasted_iota(I32, shape, axis)


def sincos(t, lg):
    q = (t + (1 << (lg - 3))) >> (lg - 2)
    r = t - (q << (lg - 2))
    th = r.astype(F32) * F32(2.0 * math.pi / (1 << lg))
    z = th * th
    s = th * (1.0 + z * (-1.0 / 6 + z * (1.0 / 120 + z * (-1.0 / 5040 + z * (1.0 / 362880)))))
    c = 1.0 + z * (-0.5 + z * (1.0 / 24 + z * (-1.0 / 720 + z * (1.0 / 40320))))
    odd = (q & 1) == 1
    cc = jnp.where(odd, s, c)
    ss = jnp.where(odd, c, s)
    return (
        jnp.where(((q + 1) & 2) != 0, -cc, cc),
        jnp.where((q & 2) != 0, -ss, ss),
    )


def split(x):
    hi = x.astype(BF16)
    return hi, (x - hi.astype(F32)).astype(BF16)


def dot(a, b):
    return lax.dot_general(a, b, (((1,), (0,)), ((), ())), preferred_element_type=F32)


def dot_t(a, b):
    return lax.dot_general(a, b, (((1,), (1,)), ((), ())), preferred_element_type=F32)


def dot3(a, bh, bl):
    n = a.shape[0]
    ah, al = split(a)
    both = dot(jnp.concatenate([ah, al], axis=0), bh)
    return both[:n] + (dot(ah, bl) + both[n:])


def kernel(
    cs_ref, vc_ref, ss_hbm, vr_hbm, vw_hbm, fac_hbm,
    cor_v, img_v, lhs_v, farh, farl, phase,
    ss_ref, vr_ref, vw_ref,
    xv, tabh, tabl, part, rec_k, snd_y, rec_y,
    snd_a, rec_a, d1, twc, tws, gai_s, gai_r, g_s, g_r,
    snd_b, rec_b, agb,
    load_sem, ks_sem, kr_sem, ys_sem, yr_sem,
    gs_sem, gr_sem, as_sem, ar_sem, cs_sem, cr_sem, bs_sem, br_sem,
    ags_sem, agr_sem, fws_sem, fwr_sem, word,
):
    r = lax.axis_index("frow")
    c = lax.axis_index("fcol")
    y = div(c, 4)
    h = rem(div(c, 2), 2)
    k = rem(c, 2)
    z = div(r, 2)
    w_lo = rem(r, 2)
    low_y = 1 - div(y, 2)
    dev_k = (r, c + 1 - 2 * k)
    y_of = [y, 3 - y, rem(y + 2, 4), rem(5 - y, 4)]
    half_of = [1 - div(yy, 2) for yy in y_of]
    h_of = [h, 1 - h]
    near = [(1, 1), (0, 1), (1, 0)]
    far = [(2, 1), (3, 1), (2, 0), (3, 0)]
    rels = near + far

    def dev_yh(rel):
        return (r, y_of[rel[0]] * 4 + h_of[rel[1]] * 2 + k)

    def group(rel):
        return rel[0] // 2

    r_peers = [rem(r + d, NR) for d in range(NR)]
    dev_r = [(rp, c) for rp in r_peers]
    by_distance = sorted(range(1, NR), key=lambda d: abs(d - NR // 2))

    def remote(src, dst, ssem, rsem, dev):
        return pltpu.make_async_remote_copy(
            src_ref=src, dst_ref=dst, send_sem=ssem, recv_sem=rsem,
            device_id=dev, device_id_type=MESH,
        )

    load = pltpu.make_async_copy(fac_hbm, xv, load_sem.at[0])
    load.start()
    small = [
        pltpu.make_async_copy(a, b, load_sem.at[i + 1])
        for i, (a, b) in enumerate([(vr_hbm, vr_ref), (vw_hbm, vw_ref), (ss_hbm, ss_ref)])
    ]
    for cp in small:
        cp.start()

    barrier = pltpu.get_barrier_semaphore()
    dev_z = [(rem(z + d, 8) * 2 + w_lo, c) for d in (1, 7, 2, 6)]
    dev_w = (r + 1 - 2 * w_lo, c)
    for dev in [dev_yh(rel) for rel in far + near] + dev_z[:2] + [dev_w, dev_k]:
        pl.semaphore_signal(barrier, inc=1, device_id=dev, device_id_type=MESH)

    f = cs_ref[0]
    off = c * LW
    pair = rem(div(y + 1, 2), 2)
    base_of = [128 * (1 - pair), 128 * pair]
    u = iota((16, 128), 0)
    place = off + iota((16, 128), 1)
    ibase = jnp.where(u < 8, base_of[0], base_of[1]) + (u & 7) * 16
    turns = [2 * ibase + 1, 2 * u, jnp.full((16, 128), 2 * f + SG - 1, I32)]
    now = [sincos((n * place) & (2 * N2 - 1), 15) for n in turns]
    step = [sincos((n * 128) & (2 * N2 - 1), 15) for n in turns]

    def table_tile(g, a, b):
        tiles = []
        for n in range(8):
            ca = a[0][g * 8 + n : g * 8 + n + 1]
            sa = a[1][g * 8 + n : g * 8 + n + 1]
            tiles.append(split(ca * b[0] - sa * b[1]) + split(sa * b[0] + ca * b[1]))
        return [
            jnp.concatenate([t[e] for t in tiles] + [t[e + 2] for t in tiles], axis=0)
            for e in range(2)
        ]

    columns = [[], []]
    waves = []
    for n in range(8):
        for g in range(2):
            columns[g].append(table_tile(g, now[0], now[1]))
        waves.append([w[0:1] * F32(1.0 / math.sqrt(N2)) for w in now[2]])
        now = [
            (ca * cb - sa * sb, sa * cb + ca * sb) for (ca, sa), (cb, sb) in zip(now, step)
        ]
    tables = [
        [jnp.concatenate([t[e] for t in columns[g]], axis=1) for e in range(2)] for g in range(2)
    ]

    load.wait()
    parts = []
    for n in range(8):
        cols = slice(n * 128, n * 128 + 128)
        pc, ps = waves[n]
        phase[0:1, cols] = pc
        phase[1:2, cols] = ps
        tiles = [[], []]
        for i in range(8):
            rows = slice(i * 16, i * 16 + 16)
            xr = xv[0, rows, cols]
            xi = xv[1, rows, cols]
            tiles[0].append(split(xr * pc + xi * ps))
            tiles[1].append(split(xi * pc - xr * ps))
        parts.append(
            [jnp.concatenate([t[e] for t in tiles[0] + tiles[1]], axis=0) for e in range(2)]
        )
    rhi, rlo = [jnp.concatenate([t[e] for t in parts], axis=1) for e in range(2)]

    def strip_group(g):
        th, tl = tables[g]
        both = dot_t(jnp.concatenate([th, tl], axis=0), rhi)
        acc = both[:256] + (dot_t(th, rlo) + both[256:])
        for hh in range(2):
            for kk in range(2):
                base = (hh * 2 + kk) * 32
                ar = acc[base : base + 32, :LH]
                ai = acc[base : base + 32, LH:]
                br = acc[128 + base : 160 + base, :LH]
                bi = acc[128 + base : 160 + base, LH:]
                part[g, kk, 0, hh, 0] = ar + bi
                part[g, kk, 0, hh, 1] = ai - br
                part[g, 1 - kk, 1, 1 - hh, 0] = ar - bi
                part[g, 1 - kk, 1, 1 - hh, 1] = ai + br

    strip_group(1)
    pl.semaphore_wait(barrier, 11)
    for dev in dev_z[:2]:
        pl.semaphore_signal(word.at[0], inc=1, device_id=dev, device_id_type=MESH)
    order = far + near + [(0, 0)]

    def cell(rel):
        return group(rel), half_of[rel[0]], h_of[rel[1]]

    def k_copy(i):
        g, sg, hh = cell(order[i])
        return remote(part.at[g, 1 - k, sg, hh], rec_k.at[g, sg, hh], ks_sem, kr_sem.at[i], dev_k)

    for i in range(4):
        k_copy(i).start()
    strip_group(0)
    for i in range(4, 8):
        k_copy(i).start()
    for i, rel in enumerate(order):
        g, sg, hh = cell(rel)
        k_copy(i).wait_recv()
        snd_y[g, sg, hh] = part[g, k, sg, hh] + rec_k[g, sg, hh]
        if i < 7:
            remote(
                snd_y.at[g, sg, hh], rec_y.at[rels.index(rel)], ys_sem, yr_sem.at[g], dev_yh(rel)
            ).start()
    pl.semaphore_wait(word.at[0], 2)
    for dev in dev_z[2:]:
        pl.semaphore_signal(word.at[1], inc=1, device_id=dev, device_id_type=MESH)

    for cp in small:
        cp.wait()
    rows_l = vr_ref[...]
    diag = iota((MAXB, MAXB), 0) == iota((MAXB, MAXB), 1)
    row_c = jnp.sum(
        jnp.where(diag, jnp.broadcast_to(rows_l, (MAXB, MAXB)).astype(F32), 0.0), axis=1, keepdims=True
    )
    row_c = row_c.astype(I32)
    wide = NR * 128
    lane = iota((32, wide), 1)
    place = ((lane >> 6) & 1) * 16 + (lane >> 7)
    place = place + low_y * (31 - 2 * place)
    sel = (iota((32, wide), 0) == place).astype(F32).astype(BF16)
    w = vw_ref[0].T
    w1 = w.astype(BF16)
    rest = w - w1.astype(F32)
    w2 = rest.astype(BF16)
    w3 = (rest - w2.astype(F32)).astype(BF16)
    wide_w = (dot(w1, sel) + dot(w2, sel)) + dot(w3, sel)
    wide_w = jnp.where((row_c >> 4) == (iota((MAXB, wide), 1) & 31), wide_w, 0.0)
    wh, wl = split(wide_w)
    low = jnp.broadcast_to(rows_l, (16, MAXB)) & 15
    lhs = ((low == iota((16, MAXB), 0)) & (iota((16, MAXB), 1) < vc_ref[0])).astype(F32).astype(BF16)
    gain = 1.0 + (dot(lhs, wh) + dot(lhs, wl))
    for i in range(NR):
        gai_s[i] = gain[:, i * 128 : (i + 1) * 128]

    def exchange(src, dst, slot, ssem, rsem):
        for d in by_distance:
            remote(src.at[r_peers[d]], dst.at[slot], ssem, rsem, dev_r[d]).start()

    def all_of(dst, ssem, rsem):
        some = dst.at[pl.ds(0, NR - 1)]
        return remote(some, some, ssem, rsem, dev_r[1])

    tabh[...] = tables[0][0]
    tabl[...] = tables[0][1]
    farh[...] = tables[1][0]
    farl[...] = tables[1][1]

    pl.semaphore_wait(word.at[1], 2)
    pl.semaphore_signal(word.at[2], inc=1, device_id=dev_w, device_id_type=MESH)

    mu = iota((16, 128), 0)
    lb = iota((16, 128), 1)

    @pl.loop(0, NR)
    def _(s):
        kf = (ss_ref[s] + mu) & (N1 - 1)
        rows = pl.ds(pl.multiple_of(s * 16, 16), 16)
        cc, sn = sincos((kf * lb) & (N1 - 1), 11)
        twc[rows, :] = cc * F32(1.0 / math.sqrt(N1))
        tws[rows, :] = sn * F32(1.0 / math.sqrt(N1))
        ca, sa = sincos((kf * (lb & 15)) & 15, 4)
        pi = (lb >> 4) & 1
        blk = lb >> 5
        for po in range(2):
            v = jnp.where(pi == 0, ca, sa) if po == 0 else jnp.where(pi == 0, -sa, ca)
            hi = v.astype(BF16).astype(F32)
            v = jnp.where(blk < 2, hi, jnp.where(blk == 2, v - hi, 0.0))
            d1[po, rows, :] = v.astype(BF16)

    pl.semaphore_wait(word.at[2], 1)
    exchange(gai_s, gai_r, r, gs_sem, gr_sem)
    gai_r[r] = gai_s[r]

    row = iota((512, 128), 0)
    col = iota((512, 128), 1)
    cc, sn = sincos(((row & 127) * (col & 31)) & 127, 7)
    pin = (row >> 7) & 1
    pout = (col >> 5) & 1
    same = (row >> 8) == (col >> 6)
    e3 = jnp.where(pin == pout, cc, jnp.where(pin == 1, sn, -sn))
    e3h, e3l = split(jnp.where(same, e3, 0.0))
    row = iota((128, 512), 0)
    col = iota((128, 512), 1)
    cc, sn = sincos(((col & 127) * (row & 31)) & 127, 7)
    pin = (row >> 5) & 1
    pout = (col >> 7) & 1
    same = (col >> 8) == (row >> 6)
    e4 = jnp.where(pin == pout, cc, jnp.where(pin == 1, -sn, sn))
    e4h, e4l = split(jnp.where(same, e4, 0.0))
    lane = iota((16, 256), 1)
    first = jnp.zeros((16, 256), I32)
    for s in range(NR):
        first = jnp.where((lane >> 4) == s, ss_ref[s], first)
    ca, sa = sincos(((first + (lane & 15)) * iota((16, 256), 0)) & 15, 4)
    d2 = jnp.concatenate(
        [jnp.concatenate([ca, -sa], axis=1), jnp.concatenate([sa, ca], axis=1)], axis=0
    )

    far_in = rec_y.at[pl.ds(3, 4)]
    near_in = rec_y.at[pl.ds(0, 3)]
    far_all = remote(far_in, far_in, ys_sem, yr_sem.at[1], dev_yh(far[0]))
    near_all = remote(near_in, near_in, ys_sem, yr_sem.at[0], dev_yh(near[0]))
    near_all.wait_recv()
    far_all.wait_recv()
    strip = (
        (snd_y[0, low_y, h] + rec_y[0]) + (rec_y[1] + rec_y[2])
    ) + ((rec_y[3] + rec_y[4]) + (rec_y[5] + rec_y[6]))
    for p in range(2):
        for q in range(2):
            snd_a[:, p * 2 + q, :] = strip[p, q * 16 : (q + 1) * 16, :]
    exchange(snd_a, rec_a, r, as_sem, ar_sem)
    rec_a[r] = snd_a[r]
    all_of(gai_r, gs_sem, gr_sem).wait_recv()
    all_of(rec_a, as_sem, ar_sem).wait_recv()

    v = jnp.concatenate(
        [jnp.concatenate([rec_a[:, p * 2 + q, :] for q in range(2)], axis=1) for p in range(2)], axis=0
    )
    vh, vl = split(v)
    stack = jnp.concatenate([vh, vl, vh, jnp.zeros_like(vh)], axis=0)
    zre = dot(d1[0], stack)
    zim = dot(d1[1], stack)
    tc = twc[...]
    ts = tws[...]
    cols = []
    for q in range(2):
        re = zre[:, q * 128 : (q + 1) * 128]
        im = zim[:, q * 128 : (q + 1) * 128]
        cols += [re * tc + im * ts, im * tc - re * ts]
    zh, zl = split(jnp.concatenate(cols, axis=1))
    wide_s = dot(zh, jnp.concatenate([e3h, e3l], axis=1))
    sub = wide_s[:, :128] + (wide_s[:, 128:] + dot(zl, e3h))
    grid = sub * gai_r[...].reshape(256, 128)
    g_s[...] = grid.reshape(NR, 16, 128)
    gh, gl = split(grid)
    vv = dot(jnp.concatenate([gh, gl], axis=1), jnp.concatenate([e4h, e4h], axis=0)) + dot(gh, e4l)
    res = []
    ims = []
    for q in range(2):
        re = vv[:, q * 256 : q * 256 + 128]
        im = vv[:, q * 256 + 128 : q * 256 + 256]
        res.append(re * tc - im * ts)
        ims.append(im * tc + re * ts)
    both = jnp.concatenate([jnp.concatenate(res, axis=1), jnp.concatenate(ims, axis=1)], axis=0)
    bh, bl = split(both)
    back = dot3(d2, bh, bl)
    for p in range(2):
        for q in range(2):
            snd_b[:, p * 2 + q, :] = back[p * 16 : (p + 1) * 16, q * 128 : (q + 1) * 128]
    exchange(snd_b, rec_b, r, bs_sem, br_sem)
    slot = r + low_y * (NR - 1 - 2 * r)
    exchange(g_s, g_r, slot, cs_sem, cr_sem)
    rec_b[r] = snd_b[r]
    g_r[slot] = g_s[r]
    all_of(rec_b, bs_sem, br_sem).wait_recv()
    for p in range(2):
        for q in range(2):
            agb[0, k, low_y, h, p, q * 16 : (q + 1) * 16, :] = rec_b[:, p * 2 + q, :]

    mine = agb.at[0, k, low_y, h]
    sends = [
        remote(mine, agb.at[group(rel), k, low_y, h], ags_sem, agr_sem.at[i], dev_yh(rel))
        for i, rel in enumerate(rels)
    ]
    for cp in sends[3:] + sends[:3]:
        cp.start()

    def block(rel, kk):
        return agb.at[group(rel), kk, half_of[rel[0]], h_of[rel[1]]]

    forwards = [
        remote(block(rel, k), block(rel, k), fws_sem, fwr_sem.at[i], dev_k)
        for i, rel in enumerate(rels + [(0, 0)])
    ]
    forwards[7].start()

    def arrive(i):
        ref = block(rels[i], k)
        remote(ref, ref, ags_sem, agr_sem.at[i], dev_yh(rels[i])).wait_recv()
        forwards[i].start()

    def forwarded(i):
        ref = block((rels + [(0, 0)])[i], 1 - k)
        remote(ref, ref, fws_sem, fwr_sem.at[i], dev_k).wait_recv()

    all_of(g_r, cs_sem, cr_sem).wait_recv()
    lane = iota((256, SG), 1)
    rowi = iota((256, SG), 0)
    gath = jnp.concatenate(split(g_r[...].reshape(256, 128)), axis=1)
    keep = (rowi & 15) == (lane & 15)
    for q in range(2):
        qq = q + low_y * (1 - 2 * q)
        for p in range(2):
            ex = ((rowi & 127) == (q * 2 + p) * 32 + (lane >> 4)).astype(F32).astype(BF16)
            wide_g = jnp.where(keep, dot(gath, ex), 0.0)
            cor_v[0, pl.ds(qq * 16, 16), p, :] = jnp.sum(wide_g.reshape(16, 16, SG), axis=1)
    for i in range(7):
        arrive(i)

    def image_lhs(g):
        er, ei, om, orr = [], [], [], []
        for hh in range(2):
            for kk in range(2):
                up = agb[g, kk, 0, hh]
                dn = agb[g, 1 - kk, 1, 1 - hh]
                er.append(up[0] + dn[0])
                ei.append(up[1] + dn[1])
                om.append(dn[1] - up[1])
                orr.append(up[0] - dn[0])
        t = [jnp.concatenate(x, axis=0).T for x in (er, om, ei, orr)]
        return jnp.concatenate(
            [jnp.concatenate(t[:2], axis=1), jnp.concatenate(t[2:], axis=1)], axis=0
        )

    for i in (7, 0, 1, 2):
        forwarded(i)
    lhs_g = image_lhs(0)
    for n in range(4):
        cols = slice(n * 256, (n + 1) * 256)
        o = dot3(lhs_g, tabh[:, cols], tabl[:, cols])
        img_v[0, :, cols] = o[:LH]
        img_v[1, :, cols] = o[LH:]
    for i in (3, 4, 5, 6):
        forwarded(i)
    lhs_v[...] = image_lhs(1)

    remote(rec_k, rec_k, ks_sem, kr_sem.at[0], dev_k).wait_send()
    remote(rec_k, rec_k, fws_sem, fwr_sem.at[0], dev_k).wait_send()
    remote(rec_y, rec_y, ys_sem, yr_sem.at[0], dev_k).wait_send()
    remote(rec_y, rec_y, ags_sem, agr_sem.at[0], dev_k).wait_send()
    all_of(gai_r, gs_sem, gr_sem).wait_send()
    all_of(rec_a, as_sem, ar_sem).wait_send()
    all_of(g_r, cs_sem, cr_sem).wait_send()
    all_of(rec_b, bs_sem, br_sem).wait_send()


def emit(cor_v, img_v, lhs_v, farh, farl, phase, cor_hbm, img_hbm, buf, sem):
    copies = [pltpu.make_async_copy(cor_v, cor_hbm, sem.at[4])]
    copies[0].start()
    lhs_g = lhs_v[...]
    for n in range(4):
        cols = slice(n * 256, (n + 1) * 256)
        o = dot3(lhs_g, farh[:, cols], farl[:, cols])
        re = img_v[0, :, cols] + o[:LH]
        im = img_v[1, :, cols] + o[LH:]
        pc = phase[0:1, cols]
        ps = phase[1:2, cols]
        buf[0, :, cols] = re * pc - im * ps
        buf[1, :, cols] = im * pc + re * ps
        cp = pltpu.make_async_copy(buf.at[:, :, cols], img_hbm.at[:, :, cols], sem.at[n])
        cp.start()
        copies.append(cp)
    for cp in copies:
        cp.wait()


def per_device(facets, column_start, subgrid_start, vis_count, vis_row, vis_weight):
    dma = pltpu.SemaphoreType.DMA
    vm = pltpu.VMEM
    smem = pl.BlockSpec(memory_space=pltpu.SMEM)
    hbm = pl.BlockSpec(memory_space=pltpu.HBM)
    vmem = pl.BlockSpec(memory_space=pltpu.VMEM)
    anym = pl.BlockSpec(memory_space=pl.ANY)
    stay = [
        pltpu.with_memory_space_constraint(x, pltpu.HBM)
        for x in (subgrid_start, vis_row, jnp.transpose(vis_weight, (0, 2, 1)), facets)
    ]
    rest = pl.pallas_call(
        kernel,
        out_shape=(
            jax.ShapeDtypeStruct((1, 32, 2, SG), F32),
            jax.ShapeDtypeStruct((2, LH, LW), F32),
            jax.ShapeDtypeStruct((2 * LH, 256), F32),
            jax.ShapeDtypeStruct((256, LW), BF16),
            jax.ShapeDtypeStruct((256, LW), BF16),
            jax.ShapeDtypeStruct((8, LW), F32),
        ),
        in_specs=[smem, smem, hbm, hbm, hbm, hbm],
        out_specs=(vmem,) * 6,
        scratch_shapes=[
            pltpu.SMEM((NR,), I32),
            vm((1, MAXB), I32),
            vm((1, 32, MAXB), F32),
            vm((2, LH, LW), F32),
            vm((256, LW), BF16),
            vm((256, LW), BF16),
            vm((2, 2, 2, 2, 2, 32, LH), F32),
            vm((2, 2, 2, 2, 32, LH), F32),
            vm((2, 2, 2, 2, 32, LH), F32),
            vm((7, 2, 32, LH), F32),
            vm((NR, 4, 128), F32),
            vm((NR, 4, 128), F32),
            vm((2, 256, 128), BF16),
            vm((256, 128), F32),
            vm((256, 128), F32),
            vm((NR, 16, 128), F32),
            vm((NR, 16, 128), F32),
            vm((NR, 16, 128), F32),
            vm((NR, 16, 128), F32),
            vm((NR, 4, 128), F32),
            vm((NR, 4, 128), F32),
            vm((2, 2, 2, 2, 2, 32, LH), F32),
            dma((4,)), dma, dma((8,)), dma, dma((2,)),
            dma, dma, dma, dma, dma, dma, dma, dma,
            dma, dma((7,)), dma, dma((8,)), pltpu.SemaphoreType.REGULAR((3,)),
        ],
        compiler_params=pltpu.CompilerParams(collective_id=0, has_side_effects=True, vmem_limit_bytes=16 * 1024 * 1024),
    )(column_start, vis_count, *stay)
    return pl.pallas_call(
        emit,
        out_shape=(
            jax.ShapeDtypeStruct((1, 32, 2, SG), F32),
            jax.ShapeDtypeStruct((2, LH, LW), F32),
        ),
        in_specs=[vmem] * 6,
        out_specs=(hbm, hbm),
        scratch_shapes=[vm((2, LH, LW), F32), dma((5,))],
        compiler_params=pltpu.CompilerParams(vmem_limit_bytes=8 * 1024 * 1024),
    )(*rest)


def solution(mesh):
    return jax.shard_map(
        per_device,
        mesh=mesh,
        in_specs=(
            P(None, "frow", "fcol"),
            P(),
            P(),
            P("frow"),
            P("frow", None),
            P("frow", None, "fcol"),
        ),
        out_specs=(P("frow", "fcol", None, None), P(None, "frow", "fcol")),
        check_vma=False,
    )
```

```python
import math

import jax
import jax.numpy as jnp
from jax import lax
from jax.experimental import pallas as pl
from jax.experimental.pallas import tpu as pltpu
from jax.sharding import PartitionSpec as P

SG = 512
MAXB = 64
NR = 16
NC = 16
N1 = 2048
N2 = 16384
LW = 1024
LH = 128

F32 = jnp.float32
BF16 = jnp.bfloat16
I32 = jnp.int32
MESH = pl.DeviceIdType.MESH


def div(a, b):
    return lax.div(a, jnp.int32(b))


def rem(a, b):
    return lax.rem(a, jnp.int32(b))


def iota(shape, axis):
    return lax.broadcasted_iota(I32, shape, axis)


def sincos(t, lg):
    q = (t + (1 << (lg - 3))) >> (lg - 2)
    r = t - (q << (lg - 2))
    th = r.astype(F32) * F32(2.0 * math.pi / (1 << lg))
    z = th * th
    s = th * (1.0 + z * (-1.0 / 6 + z * (1.0 / 120 + z * (-1.0 / 5040 + z * (1.0 / 362880)))))
    c = 1.0 + z * (-0.5 + z * (1.0 / 24 + z * (-1.0 / 720 + z * (1.0 / 40320))))
    odd = (q & 1) == 1
    cc = jnp.where(odd, s, c)
    ss = jnp.where(odd, c, s)
    return (
        jnp.where(((q + 1) & 2) != 0, -cc, cc),
        jnp.where((q & 2) != 0, -ss, ss),
    )


def split(x):
    hi = x.astype(BF16)
    return hi, (x - hi.astype(F32)).astype(BF16)


def dot(a, b):
    return lax.dot_general(a, b, (((1,), (0,)), ((), ())), preferred_element_type=F32)


def dot_t(a, b):
    return lax.dot_general(a, b, (((1,), (1,)), ((), ())), preferred_element_type=F32)


def dot3(a, bh, bl):
    n = a.shape[0]
    ah, al = split(a)
    both = dot(jnp.concatenate([ah, al], axis=0), bh)
    return both[:n] + (dot(ah, bl) + both[n:])


def kernel(
    cs_ref, vc_ref, ss_hbm, vr_hbm, vw_hbm, fac_hbm,
    cor_v, img_v, lhs_v, farh, farl, phase,
    ss_ref, vr_ref, vw_ref,
    xv, tabh, tabl, part, rec_k, snd_y, rec_y,
    snd_a, rec_a, d1, twc, tws, gai_s, gai_r, g_s, g_r,
    snd_b, rec_b, agb,
    load_sem, ks_sem, kr_sem, ys_sem, yr_sem,
    gs_sem, gr_sem, as_sem, ar_sem, cs_sem, cr_sem, bs_sem, br_sem,
    ags_sem, agr_sem, fws_sem, fwr_sem, word,
):
    r = lax.axis_index("frow")
    c = lax.axis_index("fcol")
    y = div(c, 4)
    h = rem(div(c, 2), 2)
    k = rem(c, 2)
    z = div(r, 2)
    w_lo = rem(r, 2)
    low_y = 1 - div(y, 2)
    dev_k = (r, c + 1 - 2 * k)
    y_of = [y, 3 - y, rem(y + 2, 4), rem(5 - y, 4)]
    half_of = [1 - div(yy, 2) for yy in y_of]
    h_of = [h, 1 - h]
    near = [(1, 1), (0, 1), (1, 0)]
    far = [(2, 1), (3, 1), (2, 0), (3, 0)]
    rels = near + far

    def dev_yh(rel):
        return (r, y_of[rel[0]] * 4 + h_of[rel[1]] * 2 + k)

    def group(rel):
        return rel[0] // 2

    r_peers = [rem(r + d, NR) for d in range(NR)]
    dev_r = [(rp, c) for rp in r_peers]
    by_distance = sorted(range(1, NR), key=lambda d: abs(d - NR // 2))

    def remote(src, dst, ssem, rsem, dev):
        return pltpu.make_async_remote_copy(
            src_ref=src, dst_ref=dst, send_sem=ssem, recv_sem=rsem,
            device_id=dev, device_id_type=MESH,
        )

    load = pltpu.make_async_copy(fac_hbm, xv, load_sem.at[0])
    load.start()
    small = [
        pltpu.make_async_copy(a, b, load_sem.at[i + 1])
        for i, (a, b) in enumerate([(vr_hbm, vr_ref), (vw_hbm, vw_ref), (ss_hbm, ss_ref)])
    ]
    for cp in small:
        cp.start()

    barrier = pltpu.get_barrier_semaphore()
    dev_z = [(rem(z + d, 8) * 2 + w_lo, c) for d in (1, 7, 2, 6)]
    dev_w = (r + 1 - 2 * w_lo, c)
    for dev in [dev_yh(rel) for rel in far + near] + dev_z[:2] + [dev_w, dev_k]:
        pl.semaphore_signal(barrier, inc=1, device_id=dev, device_id_type=MESH)

    f = cs_ref[0]
    off = c * LW
    pair = rem(div(y + 1, 2), 2)
    base_of = [128 * (1 - pair), 128 * pair]
    u = iota((16, 128), 0)
    place = off + iota((16, 128), 1)
    ibase = jnp.where(u < 8, base_of[0], base_of[1]) + (u & 7) * 16
    turns = [2 * ibase + 1, 2 * u, jnp.full((16, 128), 2 * f + SG - 1, I32)]
    now = [sincos((n * place) & (2 * N2 - 1), 15) for n in turns]
    step = [sincos((n * 128) & (2 * N2 - 1), 15) for n in turns]

    def table_tile(g, a, b):
        tiles = []
        for n in range(8):
            ca = a[0][g * 8 + n : g * 8 + n + 1]
            sa = a[1][g * 8 + n : g * 8 + n + 1]
            tiles.append(split(ca * b[0] - sa * b[1]) + split(sa * b[0] + ca * b[1]))
        return [
            jnp.concatenate([t[e] for t in tiles] + [t[e + 2] for t in tiles], axis=0)
            for e in range(2)
        ]

    columns = [[], []]
    waves = []
    for n in range(8):
        for g in range(2):
            columns[g].append(table_tile(g, now[0], now[1]))
        waves.append([w[0:1] * F32(1.0 / math.sqrt(N2)) for w in now[2]])
        now = [
            (ca * cb - sa * sb, sa * cb + ca * sb) for (ca, sa), (cb, sb) in zip(now, step)
        ]
    tables = [
        [jnp.concatenate([t[e] for t in columns[g]], axis=1) for e in range(2)] for g in range(2)
    ]

    load.wait()
    parts = []
    for n in range(8):
        cols = slice(n * 128, n * 128 + 128)
        pc, ps = waves[n]
        phase[0:1, cols] = pc
        phase[1:2, cols] = ps
        tiles = [[], []]
        for i in range(8):
            rows = slice(i * 16, i * 16 + 16)
            xr = xv[0, rows, cols]
            xi = xv[1, rows, cols]
            tiles[0].append(split(xr * pc + xi * ps))
            tiles[1].append(split(xi * pc - xr * ps))
        parts.append(
            [jnp.concatenate([t[e] for t in tiles[0] + tiles[1]], axis=0) for e in range(2)]
        )
    rhi, rlo = [jnp.concatenate([t[e] for t in parts], axis=1) for e in range(2)]

    def strip_group(g):
        th, tl = tables[g]
        both = dot_t(jnp.concatenate([th, tl], axis=0), rhi)
        acc = both[:256] + (dot_t(th, rlo) + both[256:])
        for hh in range(2):
            for kk in range(2):
                base = (hh * 2 + kk) * 32
                ar = acc[base : base + 32, :LH]
                ai = acc[base : base + 32, LH:]
                br = acc[128 + base : 160 + base, :LH]
                bi = acc[128 + base : 160 + base, LH:]
                part[g, kk, 0, hh, 0] = ar + bi
                part[g, kk, 0, hh, 1] = ai - br
                part[g, 1 - kk, 1, 1 - hh, 0] = ar - bi
                part[g, 1 - kk, 1, 1 - hh, 1] = ai + br

    strip_group(1)
    pl.semaphore_wait(barrier, 11)
    for dev in dev_z[:2]:
        pl.semaphore_signal(word.at[0], inc=1, device_id=dev, device_id_type=MESH)
    order = far + near + [(0, 0)]

    def cell(rel):
        return group(rel), half_of[rel[0]], h_of[rel[1]]

    def k_copy(i):
        g, sg, hh = cell(order[i])
        return remote(part.at[g, 1 - k, sg, hh], rec_k.at[g, sg, hh], ks_sem, kr_sem.at[i], dev_k)

    for i in range(4):
        k_copy(i).start()
    strip_group(0)
    for i in range(4, 8):
        k_copy(i).start()
    for i, rel in enumerate(order):
        g, sg, hh = cell(rel)
        k_copy(i).wait_recv()
        snd_y[g, sg, hh] = part[g, k, sg, hh] + rec_k[g, sg, hh]
        if i < 7:
            remote(
                snd_y.at[g, sg, hh], rec_y.at[rels.index(rel)], ys_sem, yr_sem.at[g], dev_yh(rel)
            ).start()
    pl.semaphore_wait(word.at[0], 2)
    for dev in dev_z[2:]:
        pl.semaphore_signal(word.at[1], inc=1, device_id=dev, device_id_type=MESH)

    for cp in small:
        cp.wait()
    rows_l = vr_ref[...]
    diag = iota((MAXB, MAXB), 0) == iota((MAXB, MAXB), 1)
    row_c = jnp.sum(
        jnp.where(diag, jnp.broadcast_to(rows_l, (MAXB, MAXB)).astype(F32), 0.0), axis=1, keepdims=True
    )
    row_c = row_c.astype(I32)
    wide = NR * 128
    lane = iota((32, wide), 1)
    place = ((lane >> 6) & 1) * 16 + (lane >> 7)
    place = place + low_y * (31 - 2 * place)
    sel = (iota((32, wide), 0) == place).astype(F32).astype(BF16)
    w = vw_ref[0].T
    w1 = w.astype(BF16)
    rest = w - w1.astype(F32)
    w2 = rest.astype(BF16)
    w3 = (rest - w2.astype(F32)).astype(BF16)
    wide_w = (dot(w1, sel) + dot(w2, sel)) + dot(w3, sel)
    wide_w = jnp.where((row_c >> 4) == (iota((MAXB, wide), 1) & 31), wide_w, 0.0)
    wh, wl = split(wide_w)
    low = jnp.broadcast_to(rows_l, (16, MAXB)) & 15
    lhs = ((low == iota((16, MAXB), 0)) & (iota((16, MAXB), 1) < vc_ref[0])).astype(F32).astype(BF16)
    gain = 1.0 + (dot(lhs, wh) + dot(lhs, wl))
    for i in range(NR):
        gai_s[i] = gain[:, i * 128 : (i + 1) * 128]

    def exchange(src, dst, slot, ssem, rsem):
        for d in by_distance:
            remote(src.at[r_peers[d]], dst.at[slot], ssem, rsem, dev_r[d]).start()

    def all_of(dst, ssem, rsem):
        some = dst.at[pl.ds(0, NR - 1)]
        return remote(some, some, ssem, rsem, dev_r[1])

    tabh[...] = tables[0][0]
    tabl[...] = tables[0][1]
    farh[...] = tables[1][0]
    farl[...] = tables[1][1]

    pl.semaphore_wait(word.at[1], 2)
    pl.semaphore_signal(word.at[2], inc=1, device_id=dev_w, device_id_type=MESH)

    mu = iota((16, 128), 0)
    lb = iota((16, 128), 1)

    @pl.loop(0, NR)
    def _(s):
        kf = (ss_ref[s] + mu) & (N1 - 1)
        rows = pl.ds(pl.multiple_of(s * 16, 16), 16)
        cc, sn = sincos((kf * lb) & (N1 - 1), 11)
        twc[rows, :] = cc * F32(1.0 / math.sqrt(N1))
        tws[rows, :] = sn * F32(1.0 / math.sqrt(N1))
        ca, sa = sincos((kf * (lb & 15)) & 15, 4)
        pi = (lb >> 4) & 1
        blk = lb >> 5
        for po in range(2):
            v = jnp.where(pi == 0, ca, sa) if po == 0 else jnp.where(pi == 0, -sa, ca)
            hi = v.astype(BF16).astype(F32)
            v = jnp.where(blk < 2, hi, jnp.where(blk == 2, v - hi, 0.0))
            d1[po, rows, :] = v.astype(BF16)

    pl.semaphore_wait(word.at[2], 1)
    exchange(gai_s, gai_r, r, gs_sem, gr_sem)
    gai_r[r] = gai_s[r]

    row = iota((512, 128), 0)
    col = iota((512, 128), 1)
    cc, sn = sincos(((row & 127) * (col & 31)) & 127, 7)
    pin = (row >> 7) & 1
    pout = (col >> 5) & 1
    same = (row >> 8) == (col >> 6)
    e3 = jnp.where(pin == pout, cc, jnp.where(pin == 1, sn, -sn))
    e3h, e3l = split(jnp.where(same, e3, 0.0))
    row = iota((128, 512), 0)
    col = iota((128, 512), 1)
    cc, sn = sincos(((col & 127) * (row & 31)) & 127, 7)
    pin = (row >> 5) & 1
    pout = (col >> 7) & 1
    same = (col >> 8) == (row >> 6)
    e4 = jnp.where(pin == pout, cc, jnp.where(pin == 1, -sn, sn))
    e4h, e4l = split(jnp.where(same, e4, 0.0))
    lane = iota((16, 256), 1)
    first = jnp.zeros((16, 256), I32)
    for s in range(NR):
        first = jnp.where((lane >> 4) == s, ss_ref[s], first)
    ca, sa = sincos(((first + (lane & 15)) * iota((16, 256), 0)) & 15, 4)
    d2 = jnp.concatenate(
        [jnp.concatenate([ca, -sa], axis=1), jnp.concatenate([sa, ca], axis=1)], axis=0
    )

    far_in = rec_y.at[pl.ds(3, 4)]
    near_in = rec_y.at[pl.ds(0, 3)]
    far_all = remote(far_in, far_in, ys_sem, yr_sem.at[1], dev_yh(far[0]))
    near_all = remote(near_in, near_in, ys_sem, yr_sem.at[0], dev_yh(near[0]))
    near_all.wait_recv()
    far_all.wait_recv()
    strip = (
        (snd_y[0, low_y, h] + rec_y[0]) + (rec_y[1] + rec_y[2])
    ) + ((rec_y[3] + rec_y[4]) + (rec_y[5] + rec_y[6]))
    for p in range(2):
        for q in range(2):
            snd_a[:, p * 2 + q, :] = strip[p, q * 16 : (q + 1) * 16, :]
    exchange(snd_a, rec_a, r, as_sem, ar_sem)
    rec_a[r] = snd_a[r]
    all_of(gai_r, gs_sem, gr_sem).wait_recv()
    all_of(rec_a, as_sem, ar_sem).wait_recv()

    v = jnp.concatenate(
        [jnp.concatenate([rec_a[:, p * 2 + q, :] for q in range(2)], axis=1) for p in range(2)], axis=0
    )
    vh, vl = split(v)
    stack = jnp.concatenate([vh, vl, vh, jnp.zeros_like(vh)], axis=0)
    zre = dot(d1[0], stack)
    zim = dot(d1[1], stack)
    tc = twc[...]
    ts = tws[...]
    cols = []
    for q in range(2):
        re = zre[:, q * 128 : (q + 1) * 128]
        im = zim[:, q * 128 : (q + 1) * 128]
        cols += [re * tc + im * ts, im * tc - re * ts]
    zh, zl = split(jnp.concatenate(cols, axis=1))
    wide_s = dot(zh, jnp.concatenate([e3h, e3l], axis=1))
    sub = wide_s[:, :128] + (wide_s[:, 128:] + dot(zl, e3h))
    grid = sub * gai_r[...].reshape(256, 128)
    g_s[...] = grid.reshape(NR, 16, 128)
    gh, gl = split(grid)
    vv = dot(jnp.concatenate([gh, gl], axis=1), jnp.concatenate([e4h, e4h], axis=0)) + dot(gh, e4l)
    res = []
    ims = []
    for q in range(2):
        re = vv[:, q * 256 : q * 256 + 128]
        im = vv[:, q * 256 + 128 : q * 256 + 256]
        res.append(re * tc - im * ts)
        ims.append(im * tc + re * ts)
    both = jnp.concatenate([jnp.concatenate(res, axis=1), jnp.concatenate(ims, axis=1)], axis=0)
    bh, bl = split(both)
    back = dot3(d2, bh, bl)
    for p in range(2):
        for q in range(2):
            snd_b[:, p * 2 + q, :] = back[p * 16 : (p + 1) * 16, q * 128 : (q + 1) * 128]
    exchange(snd_b, rec_b, r, bs_sem, br_sem)
    slot = r + low_y * (NR - 1 - 2 * r)
    exchange(g_s, g_r, slot, cs_sem, cr_sem)
    rec_b[r] = snd_b[r]
    g_r[slot] = g_s[r]
    all_of(rec_b, bs_sem, br_sem).wait_recv()
    for p in range(2):
        for q in range(2):
            agb[0, k, low_y, h, p, q * 16 : (q + 1) * 16, :] = rec_b[:, p * 2 + q, :]

    mine = agb.at[0, k, low_y, h]
    sends = [
        remote(mine, agb.at[group(rel), k, low_y, h], ags_sem, agr_sem.at[i], dev_yh(rel))
        for i, rel in enumerate(rels)
    ]
    for i in (3, 4, 0, 5, 1, 6, 2):
        sends[i].start()

    def block(rel, kk):
        return agb.at[group(rel), kk, half_of[rel[0]], h_of[rel[1]]]

    forwards = [
        remote(block(rel, k), block(rel, k), fws_sem, fwr_sem.at[i], dev_k)
        for i, rel in enumerate(rels + [(0, 0)])
    ]
    forwards[7].start()

    def arrive(i):
        ref = block(rels[i], k)
        remote(ref, ref, ags_sem, agr_sem.at[i], dev_yh(rels[i])).wait_recv()
        forwards[i].start()

    def forwarded(i):
        ref = block((rels + [(0, 0)])[i], 1 - k)
        remote(ref, ref, fws_sem, fwr_sem.at[i], dev_k).wait_recv()

    all_of(g_r, cs_sem, cr_sem).wait_recv()
    lane = iota((256, SG), 1)
    rowi = iota((256, SG), 0)
    gath = jnp.concatenate(split(g_r[...].reshape(256, 128)), axis=1)
    keep = (rowi & 15) == (lane & 15)
    for q in range(2):
        qq = q + low_y * (1 - 2 * q)
        for p in range(2):
            ex = ((rowi & 127) == (q * 2 + p) * 32 + (lane >> 4)).astype(F32).astype(BF16)
            wide_g = jnp.where(keep, dot(gath, ex), 0.0)
            cor_v[0, pl.ds(qq * 16, 16), p, :] = jnp.sum(wide_g.reshape(16, 16, SG), axis=1)
    for i in (2, 6, 5, 1, 0, 4, 3):
        arrive(i)

    def image_lhs(g):
        er, ei, om, orr = [], [], [], []
        for hh in range(2):
            for kk in range(2):
                up = agb[g, kk, 0, hh]
                dn = agb[g, 1 - kk, 1, 1 - hh]
                er.append(up[0] + dn[0])
                ei.append(up[1] + dn[1])
                om.append(dn[1] - up[1])
                orr.append(up[0] - dn[0])
        t = [jnp.concatenate(x, axis=0).T for x in (er, om, ei, orr)]
        return jnp.concatenate(
            [jnp.concatenate(t[:2], axis=1), jnp.concatenate(t[2:], axis=1)], axis=0
        )

    for i in (7, 0, 1, 2):
        forwarded(i)
    lhs_g = image_lhs(0)
    for n in range(4):
        cols = slice(n * 256, (n + 1) * 256)
        o = dot3(lhs_g, tabh[:, cols], tabl[:, cols])
        img_v[0, :, cols] = o[:LH]
        img_v[1, :, cols] = o[LH:]
    for i in (3, 4, 5, 6):
        forwarded(i)
    lhs_v[...] = image_lhs(1)

    remote(rec_k, rec_k, ks_sem, kr_sem.at[0], dev_k).wait_send()
    remote(rec_k, rec_k, fws_sem, fwr_sem.at[0], dev_k).wait_send()
    remote(rec_y, rec_y, ys_sem, yr_sem.at[0], dev_k).wait_send()
    remote(rec_y, rec_y, ags_sem, agr_sem.at[0], dev_k).wait_send()
    all_of(gai_r, gs_sem, gr_sem).wait_send()
    all_of(rec_a, as_sem, ar_sem).wait_send()
    all_of(g_r, cs_sem, cr_sem).wait_send()
    all_of(rec_b, bs_sem, br_sem).wait_send()


def emit(cor_v, img_v, lhs_v, farh, farl, phase, cor_hbm, img_hbm, buf, sem):
    copies = [pltpu.make_async_copy(cor_v, cor_hbm, sem.at[4])]
    copies[0].start()
    lhs_g = lhs_v[...]
    for n in range(4):
        cols = slice(n * 256, (n + 1) * 256)
        o = dot3(lhs_g, farh[:, cols], farl[:, cols])
        re = img_v[0, :, cols] + o[:LH]
        im = img_v[1, :, cols] + o[LH:]
        pc = phase[0:1, cols]
        ps = phase[1:2, cols]
        buf[0, :, cols] = re * pc - im * ps
        buf[1, :, cols] = im * pc + re * ps
        cp = pltpu.make_async_copy(buf.at[:, :, cols], img_hbm.at[:, :, cols], sem.at[n])
        cp.start()
        copies.append(cp)
    for cp in copies:
        cp.wait()


def per_device(facets, column_start, subgrid_start, vis_count, vis_row, vis_weight):
    dma = pltpu.SemaphoreType.DMA
    vm = pltpu.VMEM
    smem = pl.BlockSpec(memory_space=pltpu.SMEM)
    hbm = pl.BlockSpec(memory_space=pltpu.HBM)
    vmem = pl.BlockSpec(memory_space=pltpu.VMEM)
    anym = pl.BlockSpec(memory_space=pl.ANY)
    stay = [
        pltpu.with_memory_space_constraint(x, pltpu.HBM)
        for x in (subgrid_start, vis_row, jnp.transpose(vis_weight, (0, 2, 1)), facets)
    ]
    rest = pl.pallas_call(
        kernel,
        out_shape=(
            jax.ShapeDtypeStruct((1, 32, 2, SG), F32),
            jax.ShapeDtypeStruct((2, LH, LW), F32),
            jax.ShapeDtypeStruct((2 * LH, 256), F32),
            jax.ShapeDtypeStruct((256, LW), BF16),
            jax.ShapeDtypeStruct((256, LW), BF16),
            jax.ShapeDtypeStruct((8, LW), F32),
        ),
        in_specs=[smem, smem, hbm, hbm, hbm, hbm],
        out_specs=(vmem,) * 6,
        scratch_shapes=[
            pltpu.SMEM((NR,), I32),
            vm((1, MAXB), I32),
            vm((1, 32, MAXB), F32),
            vm((2, LH, LW), F32),
            vm((256, LW), BF16),
            vm((256, LW), BF16),
            vm((2, 2, 2, 2, 2, 32, LH), F32),
            vm((2, 2, 2, 2, 32, LH), F32),
            vm((2, 2, 2, 2, 32, LH), F32),
            vm((7, 2, 32, LH), F32),
            vm((NR, 4, 128), F32),
            vm((NR, 4, 128), F32),
            vm((2, 256, 128), BF16),
            vm((256, 128), F32),
            vm((256, 128), F32),
            vm((NR, 16, 128), F32),
            vm((NR, 16, 128), F32),
            vm((NR, 16, 128), F32),
            vm((NR, 16, 128), F32),
            vm((NR, 4, 128), F32),
            vm((NR, 4, 128), F32),
            vm((2, 2, 2, 2, 2, 32, LH), F32),
            dma((4,)), dma, dma((8,)), dma, dma((2,)),
            dma, dma, dma, dma, dma, dma, dma, dma,
            dma, dma((7,)), dma, dma((8,)), pltpu.SemaphoreType.REGULAR((3,)),
        ],
        compiler_params=pltpu.CompilerParams(collective_id=0, has_side_effects=True, vmem_limit_bytes=16 * 1024 * 1024),
    )(column_start, vis_count, *stay)
    return pl.pallas_call(
        emit,
        out_shape=(
            jax.ShapeDtypeStruct((1, 32, 2, SG), F32),
            jax.ShapeDtypeStruct((2, LH, LW), F32),
        ),
        in_specs=[vmem] * 6,
        out_specs=(hbm, hbm),
        scratch_shapes=[vm((2, LH, LW), F32), dma((5,))],
        compiler_params=pltpu.CompilerParams(vmem_limit_bytes=8 * 1024 * 1024),
    )(*rest)


def solution(mesh):
    return jax.shard_map(
        per_device,
        mesh=mesh,
        in_specs=(
            P(None, "frow", "fcol"),
            P(),
            P(),
            P("frow"),
            P("frow", None),
            P("frow", None, "fcol"),
        ),
        out_specs=(P("frow", "fcol", None, None), P(None, "frow", "fcol")),
        check_vma=False,
    )
```

```python
import math

import jax
import jax.numpy as jnp
from jax import lax
from jax.experimental import pallas as pl
from jax.experimental.pallas import tpu as pltpu
from jax.sharding import PartitionSpec as P

SG = 512
MAXB = 64
NR = 16
NC = 16
N1 = 2048
N2 = 16384
LW = 1024
LH = 128

F32 = jnp.float32
BF16 = jnp.bfloat16
I32 = jnp.int32
MESH = pl.DeviceIdType.MESH


def div(a, b):
    return lax.div(a, jnp.int32(b))


def rem(a, b):
    return lax.rem(a, jnp.int32(b))


def iota(shape, axis):
    return lax.broadcasted_iota(I32, shape, axis)


def sincos(t, lg):
    q = (t + (1 << (lg - 3))) >> (lg - 2)
    r = t - (q << (lg - 2))
    th = r.astype(F32) * F32(2.0 * math.pi / (1 << lg))
    z = th * th
    s = th * (1.0 + z * (-1.0 / 6 + z * (1.0 / 120 + z * (-1.0 / 5040 + z * (1.0 / 362880)))))
    c = 1.0 + z * (-0.5 + z * (1.0 / 24 + z * (-1.0 / 720 + z * (1.0 / 40320))))
    odd = (q & 1) == 1
    cc = jnp.where(odd, s, c)
    ss = jnp.where(odd, c, s)
    return (
        jnp.where(((q + 1) & 2) != 0, -cc, cc),
        jnp.where((q & 2) != 0, -ss, ss),
    )


def split(x):
    hi = x.astype(BF16)
    return hi, (x - hi.astype(F32)).astype(BF16)


def dot(a, b):
    return lax.dot_general(a, b, (((1,), (0,)), ((), ())), preferred_element_type=F32)


def dot_t(a, b):
    return lax.dot_general(a, b, (((1,), (1,)), ((), ())), preferred_element_type=F32)


def dot3(a, bh, bl):
    n = a.shape[0]
    ah, al = split(a)
    both = dot(jnp.concatenate([ah, al], axis=0), bh)
    return both[:n] + (dot(ah, bl) + both[n:])


def kernel(
    cs_ref, vc_ref, ss_hbm, vr_hbm, vw_hbm, fac_hbm,
    cor_v, img_v, lhs_v, farh, farl, phase,
    ss_ref, vr_ref, vw_ref,
    xv, tabh, tabl, part, rec_k, snd_y, rec_y,
    snd_a, rec_a, d1, twc, tws, gai_s, gai_r, g_s, g_r,
    snd_b, rec_b, agb,
    load_sem, ks_sem, kr_sem, ys_sem, yr_sem,
    gs_sem, gr_sem, as_sem, ar_sem, cs_sem, cr_sem, bs_sem, br_sem,
    ags_sem, agr_sem, fws_sem, fwr_sem, word,
):
    r = lax.axis_index("frow")
    c = lax.axis_index("fcol")
    y = div(c, 4)
    h = rem(div(c, 2), 2)
    k = rem(c, 2)
    z = div(r, 2)
    w_lo = rem(r, 2)
    low_y = 1 - div(y, 2)
    dev_k = (r, c + 1 - 2 * k)
    y_of = [y, 3 - y, rem(y + 2, 4), rem(5 - y, 4)]
    half_of = [1 - div(yy, 2) for yy in y_of]
    h_of = [h, 1 - h]
    near = [(1, 1), (0, 1), (1, 0)]
    far = [(2, 1), (3, 1), (2, 0), (3, 0)]
    rels = near + far

    def dev_yh(rel):
        return (r, y_of[rel[0]] * 4 + h_of[rel[1]] * 2 + k)

    def group(rel):
        return rel[0] // 2

    r_peers = [rem(r + d, NR) for d in range(NR)]
    dev_r = [(rp, c) for rp in r_peers]
    by_distance = sorted(range(1, NR), key=lambda d: abs(d - NR // 2))

    def remote(src, dst, ssem, rsem, dev):
        return pltpu.make_async_remote_copy(
            src_ref=src, dst_ref=dst, send_sem=ssem, recv_sem=rsem,
            device_id=dev, device_id_type=MESH,
        )

    load = pltpu.make_async_copy(fac_hbm, xv, load_sem.at[0])
    load.start()
    small = [
        pltpu.make_async_copy(a, b, load_sem.at[i + 1])
        for i, (a, b) in enumerate([(vr_hbm, vr_ref), (vw_hbm, vw_ref), (ss_hbm, ss_ref)])
    ]
    for cp in small:
        cp.start()

    barrier = pltpu.get_barrier_semaphore()
    dev_z = [(rem(z + d, 8) * 2 + w_lo, c) for d in (1, 7, 2, 6)]
    dev_w = (r + 1 - 2 * w_lo, c)
    for dev in [dev_yh(rel) for rel in far + near] + dev_z[:2] + [dev_w, dev_k]:
        pl.semaphore_signal(barrier, inc=1, device_id=dev, device_id_type=MESH)

    f = cs_ref[0]
    off = c * LW
    pair = rem(div(y + 1, 2), 2)
    base_of = [128 * (1 - pair), 128 * pair]
    u = iota((16, 128), 0)
    place = off + iota((16, 128), 1)
    ibase = jnp.where(u < 8, base_of[0], base_of[1]) + (u & 7) * 16
    turns = [2 * ibase + 1, 2 * u, jnp.full((16, 128), 2 * f + SG - 1, I32)]
    now = [sincos((n * place) & (2 * N2 - 1), 15) for n in turns]
    step = [sincos((n * 128) & (2 * N2 - 1), 15) for n in turns]

    def table_tile(g, a, b):
        tiles = []
        for n in range(8):
            ca = a[0][g * 8 + n : g * 8 + n + 1]
            sa = a[1][g * 8 + n : g * 8 + n + 1]
            tiles.append(split(ca * b[0] - sa * b[1]) + split(sa * b[0] + ca * b[1]))
        return [
            jnp.concatenate([t[e] for t in tiles] + [t[e + 2] for t in tiles], axis=0)
            for e in range(2)
        ]

    columns = [[], []]
    waves = []
    nears = []
    for n in range(8):
        columns[1].append(table_tile(1, now[0], now[1]))
        nears.append((now[0], now[1]))
        waves.append([w[0:1] * F32(1.0 / math.sqrt(N2)) for w in now[2]])
        now = [
            (ca * cb - sa * sb, sa * cb + ca * sb) for (ca, sa), (cb, sb) in zip(now, step)
        ]
    for near_ab in nears:
        columns[0].append(table_tile(0, *near_ab))
    tabh[...] = jnp.concatenate([t[0] for t in columns[0]], axis=1)
    tabl[...] = jnp.concatenate([t[1] for t in columns[0]], axis=1)
    load.wait()
    parts = []
    for n in range(8):
        cols = slice(n * 128, n * 128 + 128)
        pc, ps = waves[n]
        phase[0:1, cols] = pc
        phase[1:2, cols] = ps
        tiles = [[], []]
        for i in range(8):
            rows = slice(i * 16, i * 16 + 16)
            xr = xv[0, rows, cols]
            xi = xv[1, rows, cols]
            tiles[0].append(split(xr * pc + xi * ps))
            tiles[1].append(split(xi * pc - xr * ps))
        parts.append(
            [jnp.concatenate([t[e] for t in tiles[0] + tiles[1]], axis=0) for e in range(2)]
        )
    rhi, rlo = [jnp.concatenate([t[e] for t in parts], axis=1) for e in range(2)]

    tables = [
        [jnp.concatenate([t[e] for t in columns[g]], axis=1) for e in range(2)] for g in range(2)
    ]

    def strip_group(g, th, tl):
        both = dot_t(jnp.concatenate([th, tl], axis=0), rhi)
        acc = both[:256] + (dot_t(th, rlo) + both[256:])
        for hh in range(2):
            for kk in range(2):
                base = (hh * 2 + kk) * 32
                ar = acc[base : base + 32, :LH]
                ai = acc[base : base + 32, LH:]
                br = acc[128 + base : 160 + base, :LH]
                bi = acc[128 + base : 160 + base, LH:]
                part[g, kk, 0, hh, 0] = ar + bi
                part[g, kk, 0, hh, 1] = ai - br
                part[g, 1 - kk, 1, 1 - hh, 0] = ar - bi
                part[g, 1 - kk, 1, 1 - hh, 1] = ai + br

    strip_group(1, *tables[1])
    pl.semaphore_wait(barrier, 11)
    for dev in dev_z[:2]:
        pl.semaphore_signal(word.at[0], inc=1, device_id=dev, device_id_type=MESH)
    order = far + near + [(0, 0)]

    def cell(rel):
        return group(rel), half_of[rel[0]], h_of[rel[1]]

    def k_copy(i):
        g, sg, hh = cell(order[i])
        return remote(part.at[g, 1 - k, sg, hh], rec_k.at[g, sg, hh], ks_sem, kr_sem.at[i], dev_k)

    for i in range(4):
        k_copy(i).start()
    strip_group(0, tabh[...], tabl[...])
    for i in range(4, 8):
        k_copy(i).start()
    for i, rel in enumerate(order):
        g, sg, hh = cell(rel)
        k_copy(i).wait_recv()
        snd_y[g, sg, hh] = part[g, k, sg, hh] + rec_k[g, sg, hh]
        if i < 7:
            remote(
                snd_y.at[g, sg, hh], rec_y.at[rels.index(rel)], ys_sem, yr_sem.at[g], dev_yh(rel)
            ).start()
    pl.semaphore_wait(word.at[0], 2)
    for dev in dev_z[2:]:
        pl.semaphore_signal(word.at[1], inc=1, device_id=dev, device_id_type=MESH)

    for cp in small:
        cp.wait()
    rows_l = vr_ref[...]
    diag = iota((MAXB, MAXB), 0) == iota((MAXB, MAXB), 1)
    row_c = jnp.sum(
        jnp.where(diag, jnp.broadcast_to(rows_l, (MAXB, MAXB)).astype(F32), 0.0), axis=1, keepdims=True
    )
    row_c = row_c.astype(I32)
    wide = NR * 128
    lane = iota((32, wide), 1)
    place = ((lane >> 6) & 1) * 16 + (lane >> 7)
    place = place + low_y * (31 - 2 * place)
    sel = (iota((32, wide), 0) == place).astype(F32).astype(BF16)
    w = vw_ref[0].T
    w1 = w.astype(BF16)
    rest = w - w1.astype(F32)
    w2 = rest.astype(BF16)
    w3 = (rest - w2.astype(F32)).astype(BF16)
    wide_w = (dot(w1, sel) + dot(w2, sel)) + dot(w3, sel)
    wide_w = jnp.where((row_c >> 4) == (iota((MAXB, wide), 1) & 31), wide_w, 0.0)
    wh, wl = split(wide_w)
    low = jnp.broadcast_to(rows_l, (16, MAXB)) & 15
    lhs = ((low == iota((16, MAXB), 0)) & (iota((16, MAXB), 1) < vc_ref[0])).astype(F32).astype(BF16)
    gain = 1.0 + (dot(lhs, wh) + dot(lhs, wl))
    for i in range(NR):
        gai_s[i] = gain[:, i * 128 : (i + 1) * 128]

    def exchange(src, dst, slot, ssem, rsem):
        for d in by_distance:
            remote(src.at[r_peers[d]], dst.at[slot], ssem, rsem, dev_r[d]).start()

    def all_of(dst, ssem, rsem):
        some = dst.at[pl.ds(0, NR - 1)]
        return remote(some, some, ssem, rsem, dev_r[1])

    farh[...] = tables[1][0]
    farl[...] = tables[1][1]

    pl.semaphore_wait(word.at[1], 2)
    pl.semaphore_signal(word.at[2], inc=1, device_id=dev_w, device_id_type=MESH)

    mu = iota((16, 128), 0)
    lb = iota((16, 128), 1)

    @pl.loop(0, NR)
    def _(s):
        kf = (ss_ref[s] + mu) & (N1 - 1)
        rows = pl.ds(pl.multiple_of(s * 16, 16), 16)
        cc, sn = sincos((kf * lb) & (N1 - 1), 11)
        twc[rows, :] = cc * F32(1.0 / math.sqrt(N1))
        tws[rows, :] = sn * F32(1.0 / math.sqrt(N1))
        ca, sa = sincos((kf * (lb & 15)) & 15, 4)
        pi = (lb >> 4) & 1
        blk = lb >> 5
        for po in range(2):
            v = jnp.where(pi == 0, ca, sa) if po == 0 else jnp.where(pi == 0, -sa, ca)
            hi = v.astype(BF16).astype(F32)
            v = jnp.where(blk < 2, hi, jnp.where(blk == 2, v - hi, 0.0))
            d1[po, rows, :] = v.astype(BF16)

    pl.semaphore_wait(word.at[2], 1)
    exchange(gai_s, gai_r, r, gs_sem, gr_sem)
    gai_r[r] = gai_s[r]

    row = iota((512, 128), 0)
    col = iota((512, 128), 1)
    cc, sn = sincos(((row & 127) * (col & 31)) & 127, 7)
    pin = (row >> 7) & 1
    pout = (col >> 5) & 1
    same = (row >> 8) == (col >> 6)
    e3 = jnp.where(pin == pout, cc, jnp.where(pin == 1, sn, -sn))
    e3h, e3l = split(jnp.where(same, e3, 0.0))
    row = iota((128, 512), 0)
    col = iota((128, 512), 1)
    cc, sn = sincos(((col & 127) * (row & 31)) & 127, 7)
    pin = (row >> 5) & 1
    pout = (col >> 7) & 1
    same = (col >> 8) == (row >> 6)
    e4 = jnp.where(pin == pout, cc, jnp.where(pin == 1, -sn, sn))
    e4h, e4l = split(jnp.where(same, e4, 0.0))
    lane = iota((16, 256), 1)
    first = jnp.zeros((16, 256), I32)
    for s in range(NR):
        first = jnp.where((lane >> 4) == s, ss_ref[s], first)
    ca, sa = sincos(((first + (lane & 15)) * iota((16, 256), 0)) & 15, 4)
    d2 = jnp.concatenate(
        [jnp.concatenate([ca, -sa], axis=1), jnp.concatenate([sa, ca], axis=1)], axis=0
    )

    far_in = rec_y.at[pl.ds(3, 4)]
    near_in = rec_y.at[pl.ds(0, 3)]
    far_all = remote(far_in, far_in, ys_sem, yr_sem.at[1], dev_yh(far[0]))
    near_all = remote(near_in, near_in, ys_sem, yr_sem.at[0], dev_yh(near[0]))
    near_all.wait_recv()
    far_all.wait_recv()
    strip = (
        (snd_y[0, low_y, h] + rec_y[0]) + (rec_y[1] + rec_y[2])
    ) + ((rec_y[3] + rec_y[4]) + (rec_y[5] + rec_y[6]))
    for p in range(2):
        for q in range(2):
            snd_a[:, p * 2 + q, :] = strip[p, q * 16 : (q + 1) * 16, :]
    exchange(snd_a, rec_a, r, as_sem, ar_sem)
    rec_a[r] = snd_a[r]
    all_of(gai_r, gs_sem, gr_sem).wait_recv()
    all_of(rec_a, as_sem, ar_sem).wait_recv()

    v = jnp.concatenate(
        [jnp.concatenate([rec_a[:, p * 2 + q, :] for q in range(2)], axis=1) for p in range(2)], axis=0
    )
    vh, vl = split(v)
    stack = jnp.concatenate([vh, vl, vh, jnp.zeros_like(vh)], axis=0)
    zre = dot(d1[0], stack)
    zim = dot(d1[1], stack)
    tc = twc[...]
    ts = tws[...]
    cols = []
    for q in range(2):
        re = zre[:, q * 128 : (q + 1) * 128]
        im = zim[:, q * 128 : (q + 1) * 128]
        cols += [re * tc + im * ts, im * tc - re * ts]
    zh, zl = split(jnp.concatenate(cols, axis=1))
    wide_s = dot(zh, jnp.concatenate([e3h, e3l], axis=1))
    sub = wide_s[:, :128] + (wide_s[:, 128:] + dot(zl, e3h))
    grid = sub * gai_r[...].reshape(256, 128)
    g_s[...] = grid.reshape(NR, 16, 128)
    gh, gl = split(grid)
    vv = dot(jnp.concatenate([gh, gl], axis=1), jnp.concatenate([e4h, e4h], axis=0)) + dot(gh, e4l)
    res = []
    ims = []
    for q in range(2):
        re = vv[:, q * 256 : q * 256 + 128]
        im = vv[:, q * 256 + 128 : q * 256 + 256]
        res.append(re * tc - im * ts)
        ims.append(im * tc + re * ts)
    both = jnp.concatenate([jnp.concatenate(res, axis=1), jnp.concatenate(ims, axis=1)], axis=0)
    bh, bl = split(both)
    back = dot3(d2, bh, bl)
    for p in range(2):
        for q in range(2):
            snd_b[:, p * 2 + q, :] = back[p * 16 : (p + 1) * 16, q * 128 : (q + 1) * 128]
    exchange(snd_b, rec_b, r, bs_sem, br_sem)
    slot = r + low_y * (NR - 1 - 2 * r)
    exchange(g_s, g_r, slot, cs_sem, cr_sem)
    rec_b[r] = snd_b[r]
    g_r[slot] = g_s[r]
    all_of(rec_b, bs_sem, br_sem).wait_recv()
    for p in range(2):
        for q in range(2):
            agb[0, k, low_y, h, p, q * 16 : (q + 1) * 16, :] = rec_b[:, p * 2 + q, :]

    mine = agb.at[0, k, low_y, h]
    sends = [
        remote(mine, agb.at[group(rel), k, low_y, h], ags_sem, agr_sem.at[i], dev_yh(rel))
        for i, rel in enumerate(rels)
    ]
    for cp in sends[3:] + sends[:3]:
        cp.start()

    def block(rel, kk):
        return agb.at[group(rel), kk, half_of[rel[0]], h_of[rel[1]]]

    forwards = [
        remote(block(rel, k), block(rel, k), fws_sem, fwr_sem.at[i], dev_k)
        for i, rel in enumerate(rels + [(0, 0)])
    ]
    forwards[7].start()

    def arrive(i):
        ref = block(rels[i], k)
        remote(ref, ref, ags_sem, agr_sem.at[i], dev_yh(rels[i])).wait_recv()
        forwards[i].start()

    def forwarded(i):
        ref = block((rels + [(0, 0)])[i], 1 - k)
        remote(ref, ref, fws_sem, fwr_sem.at[i], dev_k).wait_recv()

    all_of(g_r, cs_sem, cr_sem).wait_recv()
    lane = iota((256, SG), 1)
    rowi = iota((256, SG), 0)
    gath = jnp.concatenate(split(g_r[...].reshape(256, 128)), axis=1)
    keep = (rowi & 15) == (lane & 15)
    for q in range(2):
        qq = q + low_y * (1 - 2 * q)
        for p in range(2):
            ex = ((rowi & 127) == (q * 2 + p) * 32 + (lane >> 4)).astype(F32).astype(BF16)
            wide_g = jnp.where(keep, dot(gath, ex), 0.0)
            cor_v[0, pl.ds(qq * 16, 16), p, :] = jnp.sum(wide_g.reshape(16, 16, SG), axis=1)
    for i in range(7):
        arrive(i)

    def image_lhs(g):
        er, ei, om, orr = [], [], [], []
        for hh in range(2):
            for kk in range(2):
                up = agb[g, kk, 0, hh]
                dn = agb[g, 1 - kk, 1, 1 - hh]
                er.append(up[0] + dn[0])
                ei.append(up[1] + dn[1])
                om.append(dn[1] - up[1])
                orr.append(up[0] - dn[0])
        t = [jnp.concatenate(x, axis=0).T for x in (er, om, ei, orr)]
        return jnp.concatenate(
            [jnp.concatenate(t[:2], axis=1), jnp.concatenate(t[2:], axis=1)], axis=0
        )

    for i in (7, 0, 1, 2):
        forwarded(i)
    lhs_g = image_lhs(0)
    for n in range(4):
        cols = slice(n * 256, (n + 1) * 256)
        o = dot3(lhs_g, tabh[:, cols], tabl[:, cols])
        img_v[0, :, cols] = o[:LH]
        img_v[1, :, cols] = o[LH:]
    for i in (3, 4, 5, 6):
        forwarded(i)
    lhs_v[...] = image_lhs(1)

    remote(rec_k, rec_k, ks_sem, kr_sem.at[0], dev_k).wait_send()
    remote(rec_k, rec_k, fws_sem, fwr_sem.at[0], dev_k).wait_send()
    remote(rec_y, rec_y, ys_sem, yr_sem.at[0], dev_k).wait_send()
    remote(rec_y, rec_y, ags_sem, agr_sem.at[0], dev_k).wait_send()
    all_of(gai_r, gs_sem, gr_sem).wait_send()
    all_of(rec_a, as_sem, ar_sem).wait_send()
    all_of(g_r, cs_sem, cr_sem).wait_send()
    all_of(rec_b, bs_sem, br_sem).wait_send()


def emit(cor_v, img_v, lhs_v, farh, farl, phase, cor_hbm, img_hbm, buf, sem):
    copies = [pltpu.make_async_copy(cor_v, cor_hbm, sem.at[4])]
    copies[0].start()
    lhs_g = lhs_v[...]
    for n in range(4):
        cols = slice(n * 256, (n + 1) * 256)
        o = dot3(lhs_g, farh[:, cols], farl[:, cols])
        re = img_v[0, :, cols] + o[:LH]
        im = img_v[1, :, cols] + o[LH:]
        pc = phase[0:1, cols]
        ps = phase[1:2, cols]
        buf[0, :, cols] = re * pc - im * ps
        buf[1, :, cols] = im * pc + re * ps
        cp = pltpu.make_async_copy(buf.at[:, :, cols], img_hbm.at[:, :, cols], sem.at[n])
        cp.start()
        copies.append(cp)
    for cp in copies:
        cp.wait()


def per_device(facets, column_start, subgrid_start, vis_count, vis_row, vis_weight):
    dma = pltpu.SemaphoreType.DMA
    vm = pltpu.VMEM
    smem = pl.BlockSpec(memory_space=pltpu.SMEM)
    hbm = pl.BlockSpec(memory_space=pltpu.HBM)
    vmem = pl.BlockSpec(memory_space=pltpu.VMEM)
    anym = pl.BlockSpec(memory_space=pl.ANY)
    stay = [
        pltpu.with_memory_space_constraint(x, pltpu.HBM)
        for x in (subgrid_start, vis_row, jnp.transpose(vis_weight, (0, 2, 1)), facets)
    ]
    rest = pl.pallas_call(
        kernel,
        out_shape=(
            jax.ShapeDtypeStruct((1, 32, 2, SG), F32),
            jax.ShapeDtypeStruct((2, LH, LW), F32),
            jax.ShapeDtypeStruct((2 * LH, 256), F32),
            jax.ShapeDtypeStruct((256, LW), BF16),
            jax.ShapeDtypeStruct((256, LW), BF16),
            jax.ShapeDtypeStruct((8, LW), F32),
        ),
        in_specs=[smem, smem, hbm, hbm, hbm, hbm],
        out_specs=(vmem,) * 6,
        scratch_shapes=[
            pltpu.SMEM((NR,), I32),
            vm((1, MAXB), I32),
            vm((1, 32, MAXB), F32),
            vm((2, LH, LW), F32),
            vm((256, LW), BF16),
            vm((256, LW), BF16),
            vm((2, 2, 2, 2, 2, 32, LH), F32),
            vm((2, 2, 2, 2, 32, LH), F32),
            vm((2, 2, 2, 2, 32, LH), F32),
            vm((7, 2, 32, LH), F32),
            vm((NR, 4, 128), F32),
            vm((NR, 4, 128), F32),
            vm((2, 256, 128), BF16),
            vm((256, 128), F32),
            vm((256, 128), F32),
            vm((NR, 16, 128), F32),
            vm((NR, 16, 128), F32),
            vm((NR, 16, 128), F32),
            vm((NR, 16, 128), F32),
            vm((NR, 4, 128), F32),
            vm((NR, 4, 128), F32),
            vm((2, 2, 2, 2, 2, 32, LH), F32),
            dma((4,)), dma, dma((8,)), dma, dma((2,)),
            dma, dma, dma, dma, dma, dma, dma, dma,
            dma, dma((7,)), dma, dma((8,)), pltpu.SemaphoreType.REGULAR((3,)),
        ],
        compiler_params=pltpu.CompilerParams(collective_id=0, has_side_effects=True, vmem_limit_bytes=16 * 1024 * 1024),
    )(column_start, vis_count, *stay)
    return pl.pallas_call(
        emit,
        out_shape=(
            jax.ShapeDtypeStruct((1, 32, 2, SG), F32),
            jax.ShapeDtypeStruct((2, LH, LW), F32),
        ),
        in_specs=[vmem] * 6,
        out_specs=(hbm, hbm),
        scratch_shapes=[vm((2, LH, LW), F32), dma((5,))],
        compiler_params=pltpu.CompilerParams(vmem_limit_bytes=8 * 1024 * 1024),
    )(*rest)


def solution(mesh):
    return jax.shard_map(
        per_device,
        mesh=mesh,
        in_specs=(
            P(None, "frow", "fcol"),
            P(),
            P(),
            P("frow"),
            P("frow", None),
            P("frow", None, "fcol"),
        ),
        out_specs=(P("frow", "fcol", None, None), P(None, "frow", "fcol")),
        check_vma=False,
    )
```

```python
import math

import jax
import jax.numpy as jnp
from jax import lax
from jax.experimental import pallas as pl
from jax.experimental.pallas import tpu as pltpu
from jax.sharding import PartitionSpec as P

SG = 512
MAXB = 64
NR = 16
NC = 16
N1 = 2048
N2 = 16384
LW = 1024
LH = 128

F32 = jnp.float32
BF16 = jnp.bfloat16
I32 = jnp.int32
MESH = pl.DeviceIdType.MESH


def div(a, b):
    return lax.div(a, jnp.int32(b))


def rem(a, b):
    return lax.rem(a, jnp.int32(b))


def iota(shape, axis):
    return lax.broadcasted_iota(I32, shape, axis)


def sincos(t, lg):
    q = (t + (1 << (lg - 3))) >> (lg - 2)
    r = t - (q << (lg - 2))
    th = r.astype(F32) * F32(2.0 * math.pi / (1 << lg))
    z = th * th
    s = th * (1.0 + z * (-1.0 / 6 + z * (1.0 / 120 + z * (-1.0 / 5040 + z * (1.0 / 362880)))))
    c = 1.0 + z * (-0.5 + z * (1.0 / 24 + z * (-1.0 / 720 + z * (1.0 / 40320))))
    odd = (q & 1) == 1
    cc = jnp.where(odd, s, c)
    ss = jnp.where(odd, c, s)
    return (
        jnp.where(((q + 1) & 2) != 0, -cc, cc),
        jnp.where((q & 2) != 0, -ss, ss),
    )


def split(x):
    hi = x.astype(BF16)
    return hi, (x - hi.astype(F32)).astype(BF16)


def dot(a, b):
    return lax.dot_general(a, b, (((1,), (0,)), ((), ())), preferred_element_type=F32)


def dot_t(a, b):
    return lax.dot_general(a, b, (((1,), (1,)), ((), ())), preferred_element_type=F32)


def dot3(a, bh, bl):
    n = a.shape[0]
    ah, al = split(a)
    both = dot(jnp.concatenate([ah, al], axis=0), bh)
    return both[:n] + (dot(ah, bl) + both[n:])


def kernel(
    cs_ref, vc_ref, ss_hbm, vr_hbm, vw_hbm, fac_hbm,
    cor_v, img_v, lhs_v, farh, farl, phase,
    ss_ref, vr_ref, vw_ref,
    xv, tabh, tabl, part, rec_k, snd_y, rec_y,
    snd_a, rec_a, d1, twc, tws, gai_s, gai_r, g_s, g_r,
    snd_b, rec_b, agb,
    load_sem, ks_sem, kr_sem, ys_sem, yr_sem,
    gs_sem, gr_sem, as_sem, ar_sem, cs_sem, cr_sem, bs_sem, br_sem,
    ags_sem, agr_sem, fws_sem, fwr_sem, word,
):
    r = lax.axis_index("frow")
    c = lax.axis_index("fcol")
    y = div(c, 4)
    h = rem(div(c, 2), 2)
    k = rem(c, 2)
    z = div(r, 2)
    w_lo = rem(r, 2)
    low_y = 1 - div(y, 2)
    dev_k = (r, c + 1 - 2 * k)
    y_of = [y, 3 - y, rem(y + 2, 4), rem(5 - y, 4)]
    half_of = [1 - div(yy, 2) for yy in y_of]
    h_of = [h, 1 - h]
    near = [(1, 1), (0, 1), (1, 0)]
    far = [(2, 1), (3, 1), (2, 0), (3, 0)]
    rels = near + far

    def dev_yh(rel):
        return (r, y_of[rel[0]] * 4 + h_of[rel[1]] * 2 + k)

    def group(rel):
        return rel[0] // 2

    r_peers = [rem(r + d, NR) for d in range(NR)]
    dev_r = [(rp, c) for rp in r_peers]
    by_distance = sorted(range(1, NR), key=lambda d: abs(d - NR // 2))

    def remote(src, dst, ssem, rsem, dev):
        return pltpu.make_async_remote_copy(
            src_ref=src, dst_ref=dst, send_sem=ssem, recv_sem=rsem,
            device_id=dev, device_id_type=MESH,
        )

    load = pltpu.make_async_copy(fac_hbm, xv, load_sem.at[0])
    load.start()
    small = [
        pltpu.make_async_copy(a, b, load_sem.at[i + 1])
        for i, (a, b) in enumerate([(vr_hbm, vr_ref), (vw_hbm, vw_ref), (ss_hbm, ss_ref)])
    ]
    for cp in small:
        cp.start()

    barrier = pltpu.get_barrier_semaphore()
    dev_z = [(rem(z + d, 8) * 2 + w_lo, c) for d in (1, 7, 2, 6)]
    dev_w = (r + 1 - 2 * w_lo, c)
    by_hops = [(3, 1), (1, 1), (0, 1), (3, 0), (1, 0)]
    for dev in [dev_yh(rel) for rel in by_hops] + dev_z[:2] + [dev_w, dev_k]:
        pl.semaphore_signal(barrier, inc=1, device_id=dev, device_id_type=MESH)

    f = cs_ref[0]
    off = c * LW
    pair = rem(div(y + 1, 2), 2)
    base_of = [128 * (1 - pair), 128 * pair]
    u = iota((16, 128), 0)
    place = off + iota((16, 128), 1)
    ibase = jnp.where(u < 8, base_of[0], base_of[1]) + (u & 7) * 16
    turns = [2 * ibase + 1, 2 * u, jnp.full((16, 128), 2 * f + SG - 1, I32)]
    now = [sincos((n * place) & (2 * N2 - 1), 15) for n in turns]
    step = [sincos((n * 128) & (2 * N2 - 1), 15) for n in turns]

    def table_tile(g, a, b):
        tiles = []
        for n in range(8):
            ca = a[0][g * 8 + n : g * 8 + n + 1]
            sa = a[1][g * 8 + n : g * 8 + n + 1]
            tiles.append(split(ca * b[0] - sa * b[1]) + split(sa * b[0] + ca * b[1]))
        return [
            jnp.concatenate([t[e] for t in tiles] + [t[e + 2] for t in tiles], axis=0)
            for e in range(2)
        ]

    columns = [[], []]
    waves = []
    nears = []
    for n in range(8):
        columns[1].append(table_tile(1, now[0], now[1]))
        nears.append((now[0], now[1]))
        waves.append([w[0:1] * F32(1.0 / math.sqrt(N2)) for w in now[2]])
        now = [
            (ca * cb - sa * sb, sa * cb + ca * sb) for (ca, sa), (cb, sb) in zip(now, step)
        ]
    for near_ab in nears:
        columns[0].append(table_tile(0, *near_ab))
    tabh[...] = jnp.concatenate([t[0] for t in columns[0]], axis=1)
    tabl[...] = jnp.concatenate([t[1] for t in columns[0]], axis=1)
    load.wait()
    parts = []
    for n in range(8):
        cols = slice(n * 128, n * 128 + 128)
        pc, ps = waves[n]
        phase[0:1, cols] = pc
        phase[1:2, cols] = ps
        tiles = [[], []]
        for i in range(8):
            rows = slice(i * 16, i * 16 + 16)
            xr = xv[0, rows, cols]
            xi = xv[1, rows, cols]
            tiles[0].append(split(xr * pc + xi * ps))
            tiles[1].append(split(xi * pc - xr * ps))
        parts.append(
            [jnp.concatenate([t[e] for t in tiles[0] + tiles[1]], axis=0) for e in range(2)]
        )
    rhi, rlo = [jnp.concatenate([t[e] for t in parts], axis=1) for e in range(2)]

    tables = [
        [jnp.concatenate([t[e] for t in columns[g]], axis=1) for e in range(2)] for g in range(2)
    ]

    def strip_group(g, th, tl):
        both = dot_t(jnp.concatenate([th, tl], axis=0), rhi)
        acc = both[:256] + (dot_t(th, rlo) + both[256:])
        for hh in range(2):
            for kk in range(2):
                base = (hh * 2 + kk) * 32
                ar = acc[base : base + 32, :LH]
                ai = acc[base : base + 32, LH:]
                br = acc[128 + base : 160 + base, :LH]
                bi = acc[128 + base : 160 + base, LH:]
                part[g, kk, 0, hh, 0] = ar + bi
                part[g, kk, 0, hh, 1] = ai - br
                part[g, 1 - kk, 1, 1 - hh, 0] = ar - bi
                part[g, 1 - kk, 1, 1 - hh, 1] = ai + br

    strip_group(1, *tables[1])
    pl.semaphore_wait(barrier, 9)
    pl.semaphore_signal(
        word.at[3], inc=1, device_id=(r, rem(y + 3, 4) * 4 + h * 2 + k), device_id_type=MESH
    )
    for dev in dev_z[:2]:
        pl.semaphore_signal(word.at[0], inc=1, device_id=dev, device_id_type=MESH)
    order = far + near + [(0, 0)]

    def cell(rel):
        return group(rel), half_of[rel[0]], h_of[rel[1]]

    def k_copy(i):
        g, sg, hh = cell(order[i])
        return remote(part.at[g, 1 - k, sg, hh], rec_k.at[g, sg, hh], ks_sem, kr_sem.at[i], dev_k)

    for i in range(4):
        k_copy(i).start()
    strip_group(0, tabh[...], tabl[...])
    for i in range(4, 8):
        k_copy(i).start()
    pl.semaphore_wait(word.at[3], 1)
    for i, rel in enumerate(order):
        g, sg, hh = cell(rel)
        k_copy(i).wait_recv()
        snd_y[g, sg, hh] = part[g, k, sg, hh] + rec_k[g, sg, hh]
        if i < 7:
            remote(
                snd_y.at[g, sg, hh], rec_y.at[rels.index(rel)], ys_sem, yr_sem.at[g], dev_yh(rel)
            ).start()
    pl.semaphore_wait(word.at[0], 2)
    for dev in dev_z[2:]:
        pl.semaphore_signal(word.at[1], inc=1, device_id=dev, device_id_type=MESH)

    for cp in small:
        cp.wait()
    rows_l = vr_ref[...]
    diag = iota((MAXB, MAXB), 0) == iota((MAXB, MAXB), 1)
    row_c = jnp.sum(
        jnp.where(diag, jnp.broadcast_to(rows_l, (MAXB, MAXB)).astype(F32), 0.0), axis=1, keepdims=True
    )
    row_c = row_c.astype(I32)
    wide = NR * 128
    lane = iota((32, wide), 1)
    place = ((lane >> 6) & 1) * 16 + (lane >> 7)
    place = place + low_y * (31 - 2 * place)
    sel = (iota((32, wide), 0) == place).astype(F32).astype(BF16)
    w = vw_ref[0].T
    w1 = w.astype(BF16)
    rest = w - w1.astype(F32)
    w2 = rest.astype(BF16)
    w3 = (rest - w2.astype(F32)).astype(BF16)
    wide_w = (dot(w1, sel) + dot(w2, sel)) + dot(w3, sel)
    wide_w = jnp.where((row_c >> 4) == (iota((MAXB, wide), 1) & 31), wide_w, 0.0)
    wh, wl = split(wide_w)
    low = jnp.broadcast_to(rows_l, (16, MAXB)) & 15
    lhs = ((low == iota((16, MAXB), 0)) & (iota((16, MAXB), 1) < vc_ref[0])).astype(F32).astype(BF16)
    gain = 1.0 + (dot(lhs, wh) + dot(lhs, wl))
    for i in range(NR):
        gai_s[i] = gain[:, i * 128 : (i + 1) * 128]

    def exchange(src, dst, slot, ssem, rsem):
        for d in by_distance:
            remote(src.at[r_peers[d]], dst.at[slot], ssem, rsem, dev_r[d]).start()

    def all_of(dst, ssem, rsem):
        some = dst.at[pl.ds(0, NR - 1)]
        return remote(some, some, ssem, rsem, dev_r[1])

    farh[...] = tables[1][0]
    farl[...] = tables[1][1]

    pl.semaphore_wait(word.at[1], 2)
    pl.semaphore_signal(word.at[2], inc=1, device_id=dev_w, device_id_type=MESH)

    mu = iota((16, 128), 0)
    lb = iota((16, 128), 1)

    @pl.loop(0, NR)
    def _(s):
        kf = (ss_ref[s] + mu) & (N1 - 1)
        rows = pl.ds(pl.multiple_of(s * 16, 16), 16)
        cc, sn = sincos((kf * lb) & (N1 - 1), 11)
        twc[rows, :] = cc * F32(1.0 / math.sqrt(N1))
        tws[rows, :] = sn * F32(1.0 / math.sqrt(N1))
        ca, sa = sincos((kf * (lb & 15)) & 15, 4)
        pi = (lb >> 4) & 1
        blk = lb >> 5
        for po in range(2):
            v = jnp.where(pi == 0, ca, sa) if po == 0 else jnp.where(pi == 0, -sa, ca)
            hi = v.astype(BF16).astype(F32)
            v = jnp.where(blk < 2, hi, jnp.where(blk == 2, v - hi, 0.0))
            d1[po, rows, :] = v.astype(BF16)

    pl.semaphore_wait(word.at[2], 1)
    exchange(gai_s, gai_r, r, gs_sem, gr_sem)
    gai_r[r] = gai_s[r]

    row = iota((512, 128), 0)
    col = iota((512, 128), 1)
    cc, sn = sincos(((row & 127) * (col & 31)) & 127, 7)
    pin = (row >> 7) & 1
    pout = (col >> 5) & 1
    same = (row >> 8) == (col >> 6)
    e3 = jnp.where(pin == pout, cc, jnp.where(pin == 1, sn, -sn))
    e3h, e3l = split(jnp.where(same, e3, 0.0))
    row = iota((128, 512), 0)
    col = iota((128, 512), 1)
    cc, sn = sincos(((col & 127) * (row & 31)) & 127, 7)
    pin = (row >> 5) & 1
    pout = (col >> 7) & 1
    same = (col >> 8) == (row >> 6)
    e4 = jnp.where(pin == pout, cc, jnp.where(pin == 1, -sn, sn))
    e4h, e4l = split(jnp.where(same, e4, 0.0))
    lane = iota((16, 256), 1)
    first = jnp.zeros((16, 256), I32)
    for s in range(NR):
        first = jnp.where((lane >> 4) == s, ss_ref[s], first)
    ca, sa = sincos(((first + (lane & 15)) * iota((16, 256), 0)) & 15, 4)
    d2 = jnp.concatenate(
        [jnp.concatenate([ca, -sa], axis=1), jnp.concatenate([sa, ca], axis=1)], axis=0
    )

    far_in = rec_y.at[pl.ds(3, 4)]
    near_in = rec_y.at[pl.ds(0, 3)]
    far_all = remote(far_in, far_in, ys_sem, yr_sem.at[1], dev_yh(far[0]))
    near_all = remote(near_in, near_in, ys_sem, yr_sem.at[0], dev_yh(near[0]))
    near_all.wait_recv()
    far_all.wait_recv()
    strip = (
        (snd_y[0, low_y, h] + rec_y[0]) + (rec_y[1] + rec_y[2])
    ) + ((rec_y[3] + rec_y[4]) + (rec_y[5] + rec_y[6]))
    for p in range(2):
        for q in range(2):
            snd_a[:, p * 2 + q, :] = strip[p, q * 16 : (q + 1) * 16, :]
    exchange(snd_a, rec_a, r, as_sem, ar_sem)
    rec_a[r] = snd_a[r]
    all_of(gai_r, gs_sem, gr_sem).wait_recv()
    all_of(rec_a, as_sem, ar_sem).wait_recv()

    v = jnp.concatenate(
        [jnp.concatenate([rec_a[:, p * 2 + q, :] for q in range(2)], axis=1) for p in range(2)], axis=0
    )
    vh, vl = split(v)
    stack = jnp.concatenate([vh, vl, vh, jnp.zeros_like(vh)], axis=0)
    zre = dot(d1[0], stack)
    zim = dot(d1[1], stack)
    tc = twc[...]
    ts = tws[...]
    cols = []
    for q in range(2):
        re = zre[:, q * 128 : (q + 1) * 128]
        im = zim[:, q * 128 : (q + 1) * 128]
        cols += [re * tc + im * ts, im * tc - re * ts]
    zh, zl = split(jnp.concatenate(cols, axis=1))
    wide_s = dot(zh, jnp.concatenate([e3h, e3l], axis=1))
    sub = wide_s[:, :128] + (wide_s[:, 128:] + dot(zl, e3h))
    grid = sub * gai_r[...].reshape(256, 128)
    g_s[...] = grid.reshape(NR, 16, 128)
    gh, gl = split(grid)
    vv = dot(jnp.concatenate([gh, gl], axis=1), jnp.concatenate([e4h, e4h], axis=0)) + dot(gh, e4l)
    res = []
    ims = []
    for q in range(2):
        re = vv[:, q * 256 : q * 256 + 128]
        im = vv[:, q * 256 + 128 : q * 256 + 256]
        res.append(re * tc - im * ts)
        ims.append(im * tc + re * ts)
    both = jnp.concatenate([jnp.concatenate(res, axis=1), jnp.concatenate(ims, axis=1)], axis=0)
    bh, bl = split(both)
    back = dot3(d2, bh, bl)
    for p in range(2):
        for q in range(2):
            snd_b[:, p * 2 + q, :] = back[p * 16 : (p + 1) * 16, q * 128 : (q + 1) * 128]
    exchange(snd_b, rec_b, r, bs_sem, br_sem)
    slot = r + low_y * (NR - 1 - 2 * r)
    exchange(g_s, g_r, slot, cs_sem, cr_sem)
    rec_b[r] = snd_b[r]
    g_r[slot] = g_s[r]
    all_of(rec_b, bs_sem, br_sem).wait_recv()
    for p in range(2):
        for q in range(2):
            agb[0, k, low_y, h, p, q * 16 : (q + 1) * 16, :] = rec_b[:, p * 2 + q, :]

    mine = agb.at[0, k, low_y, h]
    sends = [
        remote(mine, agb.at[group(rel), k, low_y, h], ags_sem, agr_sem.at[i], dev_yh(rel))
        for i, rel in enumerate(rels)
    ]
    for cp in sends[3:] + sends[:3]:
        cp.start()

    def block(rel, kk):
        return agb.at[group(rel), kk, half_of[rel[0]], h_of[rel[1]]]

    forwards = [
        remote(block(rel, k), block(rel, k), fws_sem, fwr_sem.at[i], dev_k)
        for i, rel in enumerate(rels + [(0, 0)])
    ]
    forwards[7].start()

    def arrive(i):
        ref = block(rels[i], k)
        remote(ref, ref, ags_sem, agr_sem.at[i], dev_yh(rels[i])).wait_recv()
        forwards[i].start()

    def forwarded(i):
        ref = block((rels + [(0, 0)])[i], 1 - k)
        remote(ref, ref, fws_sem, fwr_sem.at[i], dev_k).wait_recv()

    all_of(g_r, cs_sem, cr_sem).wait_recv()
    lane = iota((256, SG), 1)
    rowi = iota((256, SG), 0)
    gath = jnp.concatenate(split(g_r[...].reshape(256, 128)), axis=1)
    keep = (rowi & 15) == (lane & 15)
    for q in range(2):
        qq = q + low_y * (1 - 2 * q)
        for p in range(2):
            ex = ((rowi & 127) == (q * 2 + p) * 32 + (lane >> 4)).astype(F32).astype(BF16)
            wide_g = jnp.where(keep, dot(gath, ex), 0.0)
            cor_v[0, pl.ds(qq * 16, 16), p, :] = jnp.sum(wide_g.reshape(16, 16, SG), axis=1)
    for i in range(7):
        arrive(i)

    def image_lhs(g):
        er, ei, om, orr = [], [], [], []
        for hh in range(2):
            for kk in range(2):
                up = agb[g, kk, 0, hh]
                dn = agb[g, 1 - kk, 1, 1 - hh]
                er.append(up[0] + dn[0])
                ei.append(up[1] + dn[1])
                om.append(dn[1] - up[1])
                orr.append(up[0] - dn[0])
        t = [jnp.concatenate(x, axis=0).T for x in (er, om, ei, orr)]
        return jnp.concatenate(
            [jnp.concatenate(t[:2], axis=1), jnp.concatenate(t[2:], axis=1)], axis=0
        )

    for i in (7, 0, 1, 2):
        forwarded(i)
    lhs_g = image_lhs(0)
    for n in range(4):
        cols = slice(n * 256, (n + 1) * 256)
        o = dot3(lhs_g, tabh[:, cols], tabl[:, cols])
        img_v[0, :, cols] = o[:LH]
        img_v[1, :, cols] = o[LH:]
    for i in (3, 4, 5, 6):
        forwarded(i)
    lhs_v[...] = image_lhs(1)

    remote(rec_k, rec_k, ks_sem, kr_sem.at[0], dev_k).wait_send()
    remote(rec_k, rec_k, fws_sem, fwr_sem.at[0], dev_k).wait_send()
    remote(rec_y, rec_y, ys_sem, yr_sem.at[0], dev_k).wait_send()
    remote(rec_y, rec_y, ags_sem, agr_sem.at[0], dev_k).wait_send()
    all_of(gai_r, gs_sem, gr_sem).wait_send()
    all_of(rec_a, as_sem, ar_sem).wait_send()
    all_of(g_r, cs_sem, cr_sem).wait_send()
    all_of(rec_b, bs_sem, br_sem).wait_send()


def emit(cor_v, img_v, lhs_v, farh, farl, phase, cor_hbm, img_hbm, buf, sem):
    copies = [pltpu.make_async_copy(cor_v, cor_hbm, sem.at[4])]
    copies[0].start()
    lhs_g = lhs_v[...]
    for n in range(4):
        cols = slice(n * 256, (n + 1) * 256)
        o = dot3(lhs_g, farh[:, cols], farl[:, cols])
        re = img_v[0, :, cols] + o[:LH]
        im = img_v[1, :, cols] + o[LH:]
        pc = phase[0:1, cols]
        ps = phase[1:2, cols]
        buf[0, :, cols] = re * pc - im * ps
        buf[1, :, cols] = im * pc + re * ps
        cp = pltpu.make_async_copy(buf.at[:, :, cols], img_hbm.at[:, :, cols], sem.at[n])
        cp.start()
        copies.append(cp)
    for cp in copies:
        cp.wait()


def per_device(facets, column_start, subgrid_start, vis_count, vis_row, vis_weight):
    dma = pltpu.SemaphoreType.DMA
    vm = pltpu.VMEM
    smem = pl.BlockSpec(memory_space=pltpu.SMEM)
    hbm = pl.BlockSpec(memory_space=pltpu.HBM)
    vmem = pl.BlockSpec(memory_space=pltpu.VMEM)
    anym = pl.BlockSpec(memory_space=pl.ANY)
    stay = [
        pltpu.with_memory_space_constraint(x, pltpu.HBM)
        for x in (subgrid_start, vis_row, jnp.transpose(vis_weight, (0, 2, 1)), facets)
    ]
    rest = pl.pallas_call(
        kernel,
        out_shape=(
            jax.ShapeDtypeStruct((1, 32, 2, SG), F32),
            jax.ShapeDtypeStruct((2, LH, LW), F32),
            jax.ShapeDtypeStruct((2 * LH, 256), F32),
            jax.ShapeDtypeStruct((256, LW), BF16),
            jax.ShapeDtypeStruct((256, LW), BF16),
            jax.ShapeDtypeStruct((8, LW), F32),
        ),
        in_specs=[smem, smem, hbm, hbm, hbm, hbm],
        out_specs=(vmem,) * 6,
        scratch_shapes=[
            pltpu.SMEM((NR,), I32),
            vm((1, MAXB), I32),
            vm((1, 32, MAXB), F32),
            vm((2, LH, LW), F32),
            vm((256, LW), BF16),
            vm((256, LW), BF16),
            vm((2, 2, 2, 2, 2, 32, LH), F32),
            vm((2, 2, 2, 2, 32, LH), F32),
            vm((2, 2, 2, 2, 32, LH), F32),
            vm((7, 2, 32, LH), F32),
            vm((NR, 4, 128), F32),
            vm((NR, 4, 128), F32),
            vm((2, 256, 128), BF16),
            vm((256, 128), F32),
            vm((256, 128), F32),
            vm((NR, 16, 128), F32),
            vm((NR, 16, 128), F32),
            vm((NR, 16, 128), F32),
            vm((NR, 16, 128), F32),
            vm((NR, 4, 128), F32),
            vm((NR, 4, 128), F32),
            vm((2, 2, 2, 2, 2, 32, LH), F32),
            dma((4,)), dma, dma((8,)), dma, dma((2,)),
            dma, dma, dma, dma, dma, dma, dma, dma,
            dma, dma((7,)), dma, dma((8,)), pltpu.SemaphoreType.REGULAR((4,)),
        ],
        compiler_params=pltpu.CompilerParams(collective_id=0, has_side_effects=True, vmem_limit_bytes=16 * 1024 * 1024),
    )(column_start, vis_count, *stay)
    return pl.pallas_call(
        emit,
        out_shape=(
            jax.ShapeDtypeStruct((1, 32, 2, SG), F32),
            jax.ShapeDtypeStruct((2, LH, LW), F32),
        ),
        in_specs=[vmem] * 6,
        out_specs=(hbm, hbm),
        scratch_shapes=[vm((2, LH, LW), F32), dma((5,))],
        compiler_params=pltpu.CompilerParams(vmem_limit_bytes=8 * 1024 * 1024),
    )(*rest)


def solution(mesh):
    return jax.shard_map(
        per_device,
        mesh=mesh,
        in_specs=(
            P(None, "frow", "fcol"),
            P(),
            P(),
            P("frow"),
            P("frow", None),
            P("frow", None, "fcol"),
        ),
        out_specs=(P("frow", "fcol", None, None), P(None, "frow", "fcol")),
        check_vma=False,
    )
```
